512 devices in a mesh: gx: 64 (over x, y, z_lo), gy: 8 (over z_hi, core).
Axes of the slice: x: 4, y: 4, z: 16 (z_hi: 4, z_lo: 4; z = z_hi * 4 + z_lo), core: 2. Of those that a mesh axis runs over, the one named last changes fastest.
Arguments:
- displacement: float32 [3, 1536, 192, 128], P(None, 'gx', 'gy'), may hold values from -25 to 25
- velocity: float32 [3, 1536, 192, 128], P(None, 'gx', 'gy'), may hold values from -6 to 6
- history: float32 [1536, 192, 128], P('gx', 'gy'), may hold values from 1 to 10
- zone: int32 [1536, 192, 128], P('gx', 'gy'), may hold values from 0 to 7
- zone_modulus: float32 [8], replicated, may hold values from 0.5 to 2
- zone_threshold: float32 [8], replicated, may hold values from 0.5 to 4
- zone_density: float32 [8], replicated, may hold values from 0.5 to 2
Outputs:
- new_displacement: float32 [3, 1536, 192, 128], P(None, 'gx', 'gy')
- new_velocity: float32 [3, 1536, 192, 128], P(None, 'gx', 'gy')
- new_history: float32 [1536, 192, 128], P('gx', 'gy')
The draws below stay inside these ranges and needn't reach their ends.
All inputs are finite; a program needn't handle non-finite values.
Results may differ from the reference program's by a relative error of at most 0.000068.
Values sent between devices are 32-bit elements; how exact they have to be, the bound alone decides.
A program may use at most 64 MiB of HBM per device.

```python
import math
import jax
import jax.numpy as jnp
from jax import lax

RADIUS = 24
ZONES = 8
NX = 1536
NY = 192
NZ = 128


def slab_factor(starts, lengths, count):
    position = lax.broadcasted_iota(jnp.int32, (starts.shape[0], count), 1)
    inside = (position >= starts[:, None]) & (position < starts[:, None] + lengths[:, None])
    return jnp.where(inside, 1.0, 0.0).astype(jnp.float32)


def crack_family(subkey, number, normal_count, side_count, depth):
    pieces = jax.random.split(subkey, 7)
    normal_start = jax.random.randint(pieces[0], (number,), 0, normal_count - 2)
    normal_length = jnp.full((number,), 3, jnp.int32)
    side_length = jax.random.randint(pieces[1], (number,), min(RADIUS, side_count), min(6 * RADIUS, side_count) + 1)
    side_start = jax.random.randint(pieces[2], (number,), 0, side_count - side_length + 1)
    depth_length = jax.random.randint(pieces[3], (number,), max(1, depth // 4), depth + 1)
    depth_start = jax.random.randint(pieces[4], (number,), 0, depth - depth_length + 1)
    magnitude = jax.random.uniform(pieces[5], (number, 3), jnp.float32, 10.0, 25.0)
    flipped = jax.random.bernoulli(pieces[6], 0.5, (number, 3))
    amplitude = jnp.where(flipped, -magnitude, magnitude)
    normal_factor = slab_factor(normal_start, normal_length, normal_count)
    side_factor = slab_factor(side_start, side_length, side_count)
    depth_factor = slab_factor(depth_start, depth_length, depth)
    return (normal_factor, side_factor, depth_factor, amplitude)


def draw_displacement(key, part):
    subkeys = jax.random.split(jax.random.fold_in(key, 31), 4)
    number = max(1, NX // 12)
    first_x, first_y, first_z, first_amp = crack_family(subkeys[0], number, NX, NY, NZ)
    second_y, second_x, second_z, second_amp = crack_family(subkeys[1], number, NY, NX, NZ)
    along_x = jnp.concatenate([first_x, second_x], axis=0)
    along_y = jnp.concatenate([first_y, second_y], axis=0)
    along_z = jnp.concatenate([first_z, second_z], axis=0)
    amplitude = jnp.concatenate([first_amp, second_amp], axis=0)
    plane = along_x[:, :, None] * along_y[:, None, :]
    cracks = jnp.stack([jnp.einsum('cxy,cz->xyz', plane * amplitude[:, j, None, None], along_z, precision=lax.Precision.HIGHEST) for j in range(3)])
    background = jax.random.normal(subkeys[3], (3, NX, NY, NZ), jnp.float32)
    return jnp.clip(background + cracks, -25.0, 25.0).astype(jnp.float32)


def with_ends(array, stream_key, low, high):
    dims = array.shape
    spot = [jax.random.randint(jax.random.fold_in(stream_key, axis), (), 0, dims[axis]) for axis in range(len(dims))]
    array = array.at[tuple(spot)].set(low)
    longest = dims.index(max(dims))
    spot[longest] = (spot[longest] + 1) % dims[longest]
    return array.at[tuple(spot)].set(high)


def block_scale(rng, shape, cuts, least, largest):
    factor_of = 1.0
    for axis_at, shards_of in cuts:
        draws = jax.random.uniform(jax.random.fold_in(jax.random.fold_in(rng, 6), axis_at), (shards_of,), jnp.float32, least / len(cuts), largest / len(cuts))
        factor_of = factor_of * jnp.repeat(jnp.exp(draws), shape[axis_at] // shards_of).reshape((-1,) + (1,) * (len(shape) - 1 - axis_at))
    return factor_of


def bell_draw(own_key, shape, width, limit, cuts=(), dtype=jnp.bfloat16):
    factor_of = block_scale(own_key, shape, cuts, -0.22, 0.18) if cuts else 1.0
    entries = jax.random.normal(own_key, shape, jnp.float32) * width * factor_of
    return jnp.minimum(jnp.maximum(entries, -limit), limit).astype(dtype)


def setup_inputs(seed: int = 0) -> dict:
    arg_keys = jax.random.split(jax.random.key(seed), 8)
    displacement = draw_displacement(jax.random.fold_in(arg_keys[7], 71), 0)
    velocity = bell_draw(arg_keys[1], (3, NX, NY, NZ), 1.0, 6.0, ((1, 64), (2, 8)), jnp.float32)
    history = jnp.clip(jnp.exp(math.log(10.0) - 2.3025851 * jax.random.uniform(arg_keys[2], (NX, NY, NZ), jnp.float32) ** block_scale(arg_keys[2], (NX, NY, NZ), ((0, 64), (1, 8)), -0.2, 0.2)), 1.0, 10.0)
    zone = with_ends(jax.random.randint(arg_keys[3], (NX, NY, NZ), 0, ZONES), jax.random.fold_in(arg_keys[3], 1), 0, ZONES - 1).astype(jnp.int32)
    zone_modulus = jnp.clip(jnp.exp(jax.random.uniform(arg_keys[4], (ZONES,), jnp.float32, math.log(0.5), math.log(2.0))), 0.5, 2.0)
    zone_threshold = jnp.clip(jnp.exp(jax.random.uniform(arg_keys[5], (ZONES,), jnp.float32, math.log(0.5), math.log(4.0))), 0.5, 4.0)
    zone_density = jnp.clip(jnp.exp(jax.random.uniform(arg_keys[6], (ZONES,), jnp.float32, math.log(0.5), math.log(2.0))), 0.5, 2.0)
    return {"displacement": displacement, "velocity": velocity, "history": history, "zone": zone, "zone_modulus": zone_modulus, "zone_threshold": zone_threshold, "zone_density": zone_density}


def ahead(field, axis):
    widths = tuple(((0, 1) if k == axis else (0, 0) for k in range(field.ndim)))
    return lax.slice_in_dim(jnp.pad(field, widths), 1, field.shape[axis] + 1, axis=axis)

def behind(field, axis):
    widths = tuple(((1, 0) if k == axis else (0, 0) for k in range(field.ndim)))
    return lax.slice_in_dim(jnp.pad(field, widths), 0, field.shape[axis], axis=axis)

def smooth_axis(field, axis):
    count = field.shape[axis]
    widths = tuple(((RADIUS, RADIUS) if k == axis else (0, 0) for k in range(field.ndim)))
    padded = jnp.pad(field, widths)
    total = jnp.zeros_like(field)
    for offset in range(-RADIUS, RADIUS + 1):
        weight = 1.0 - 0.5 * (offset / RADIUS) ** 2
        total = total + weight * lax.slice_in_dim(padded, RADIUS + offset, RADIUS + offset + count, axis=axis)
    return total

def coverage(count):
    place = jnp.arange(count)
    total = jnp.zeros((count,), jnp.float32)
    for offset in range(-RADIUS, RADIUS + 1):
        weight = 1.0 - 0.5 * (offset / RADIUS) ** 2
        inside = (place + offset >= 0) & (place + offset < count)
        total = total + jnp.where(inside, weight, 0.0).astype(jnp.float32)
    return total

def reference(displacement, velocity, history, zone, zone_modulus, zone_threshold, zone_density):
    grads = [[ahead(displacement[j], i) - displacement[j] for j in range(3)] for i in range(3)]
    strain = [[0.5 * (grads[i][j] + grads[j][i]) for j in range(3)] for i in range(3)]
    squares = strain[0][0] ** 2 + strain[1][1] ** 2 + strain[2][2] ** 2
    squares = squares + 2.0 * (strain[0][1] ** 2 + strain[0][2] ** 2 + strain[1][2] ** 2)
    equivalent = jnp.sqrt(squares)
    smoothed = smooth_axis(smooth_axis(smooth_axis(equivalent, 2), 0), 1)
    denom = coverage(NX)[:, None, None] * coverage(NY)[None, :, None] * coverage(NZ)[None, None, :]
    average = smoothed / denom
    new_history = jnp.maximum(history, average)
    modulus = zone_modulus[zone]
    threshold = zone_threshold[zone]
    density = zone_density[zone]
    bounded = jnp.maximum(new_history, threshold)
    damage = 1.0 - threshold / bounded * jnp.exp(-0.5 * (bounded - threshold))
    trace = strain[0][0] + strain[1][1] + strain[2][2]
    intact = 1.0 - damage
    stress = [[intact * ((modulus * trace if i == j else 0.0) + 2.0 * modulus * strain[i][j]) for j in range(3)] for i in range(3)]
    force = [sum((stress[i][j] - behind(stress[i][j], i) for i in range(3))) for j in range(3)]
    new_velocity = velocity + 0.1 * jnp.stack(force) / density[None]
    new_displacement = displacement + 0.1 * new_velocity
    return (new_displacement, new_velocity, new_history)
```

```python
import functools

import jax
import jax.numpy as jnp
from jax import lax
from jax.experimental import pallas as pl
from jax.experimental.pallas import tpu as pltpu
from jax.sharding import PartitionSpec as P

RADIUS = 24
TAPS = 2 * RADIUS + 1
N = 24
DEPTH = 128
CH = 8
F32 = jnp.float32
MESH = pl.DeviceIdType.MESH
HIGHEST = lax.Precision.HIGHEST

WEIGHT = [1.0 - 0.5 * ((t - RADIUS) / RADIUS) ** 2 for t in range(TAPS)]


def ramp(a):
    return (a * (a + 1) * (2 * a + 1)).astype(F32) * (1.0 / 6.0)


def coverage(place, total):
    low = jnp.minimum(place, RADIUS)
    high = jnp.minimum(total - 1 - place, RADIUS)
    return (low + high + 1).astype(F32) - (ramp(low) + ramp(high)) * (0.5 / RADIUS**2)


def band(offset):
    ratio = offset.astype(F32) * (1.0 / RADIUS)
    return jnp.where(jnp.abs(offset) <= RADIUS, 1.0 - 0.5 * ratio * ratio, 0.0)


def lookup(bits, table):
    level = [table[k] for k in range(8)]
    for bit in bits:
        level = [jnp.where(bit, level[k + 1], level[k]) for k in range(0, len(level), 2)]
    return level[0]


def taps(rows):
    total = rows(RADIUS)
    for t in range(RADIUS):
        total = total + WEIGHT[t] * (rows(t) + rows(TAPS - 1 - t))
    return total


def kernel(
    ngx, ngy,
    disp, vel, hist, zone, modulus, threshold, density,
    nd_out, nv_out, nh_out,
    de, v, h, z, fys, fy, er, e, yb, out, xr, u, tm, rm, ix, iy, pxs, px, pys, py, pyi, nd, nv, nh,
    lsem, ssem, rsem,
):
    gx = lax.axis_index("gx")
    gy = lax.axis_index("gy")
    where_am = {"gx": gx, "gy": gy}
    count = {"gx": ngx, "gy": ngy}

    def reach(axis, step):
        place = where_am[axis] + step
        return (place >= 0) & (place < count[axis])

    local = [
        pltpu.make_async_copy(disp, de.at[:, pl.ds(0, N), pl.ds(0, N), :], lsem.at[0]),
        pltpu.make_async_copy(hist, h, lsem.at[1]),
        pltpu.make_async_copy(zone, z, lsem.at[2]),
        pltpu.make_async_copy(vel, v, lsem.at[3]),
    ]
    for copy in local:
        copy.start()

    barrier = pltpu.get_barrier_semaphore()
    partners = jnp.int32(0)
    for axis in ("gx", "gy"):
        for step in (-2, -1, 1, 2):
            ok = reach(axis, step)
            partners = partners + jnp.where(ok, 1, 0)

            @pl.when(ok)
            def _(axis=axis, step=step):
                pl.semaphore_signal(
                    barrier, inc=1, device_id={axis: where_am[axis] + step}, device_id_type=MESH
                )

    made = []

    def remote(src, dst, axis, step):
        k = len(made)
        copy = pltpu.make_async_remote_copy(
            src_ref=src,
            dst_ref=dst,
            send_sem=ssem.at[k],
            recv_sem=rsem.at[k],
            device_id={axis: where_am[axis] + step},
            device_id_type=MESH,
        )
        made.append((copy, axis, step))
        return k

    def start(k):
        copy, axis, step = made[k]
        pl.when(reach(axis, step))(copy.start)

    def arrived(k):
        copy, axis, step = made[k]
        pl.when(reach(axis, -step))(copy.wait_recv)

    def left(k):
        copy, axis, step = made[k]
        pl.when(reach(axis, step))(copy.wait_send)

    def rows(ref, first, number):
        return ref.at[pl.ds(first * N, number * N), :]

    front_x = remote(de.at[:, 0, pl.ds(0, N), :], de.at[:, N, pl.ds(0, N), :], "gx", -1)
    front_y = remote(fys, fy, "gy", -1)
    part_x = []
    for c in range(3):
        span = pl.ds(c * CH, CH)
        src = e.at[pl.ds(25, 23), span, :]
        part_x.append(
            (
                remote(src, e.at[pl.ds(1, 23), span, :], "gx", 1),
                remote(src, e.at[pl.ds(49, 23), span, :], "gx", -1),
            )
        )
    last_x = (
        remote(e.at[48], e.at[24], "gx", 1),
        remote(e.at[48], e.at[72], "gx", -1),
        remote(e.at[48], e.at[0], "gx", 2),
    )
    part_y = []
    for c in range(3):
        src = rows(yb, 25 + c * CH, CH)
        part_y.append(
            (
                remote(src, rows(yb, 1 + c * CH, CH), "gy", 1),
                remote(src, rows(yb, 49 + c * CH, CH), "gy", -1),
            )
        )
    edge_y = (
        remote(rows(yb, 48, 1), rows(yb, 0, 1), "gy", 2),
        remote(xr.at[pl.ds(N, N), :], xr.at[pl.ds(0, N), :], "gy", 1),
        remote(xr.at[pl.ds(N, N), :], xr.at[pl.ds(2 * N, N), :], "gy", -1),
    )
    face_x = remote(pxs, px, "gx", 1)
    face_y = remote(pys, py, "gy", 1)

    zeros = functools.partial(jnp.zeros, dtype=F32)

    @pl.when(gx == 0)
    def _():
        e[pl.ds(0, 25)] = zeros((25, N, DEPTH))
        px[0:3] = zeros((3, N, DEPTH))
        px[3:5] = zeros((2, N, DEPTH)) + 1.0

    @pl.when(gx == 1)
    def _():
        e[0] = zeros((N, DEPTH))

    @pl.when(gx == ngx - 1)
    def _():
        e[pl.ds(49, 24)] = zeros((24, N, DEPTH))
        for j in range(3):
            de[j, N, 0:N, :] = zeros((N, DEPTH))

    @pl.when(gy == 0)
    def _():
        yb[0 : 25 * N] = zeros((25 * N, DEPTH))
        xr[0:N] = zeros((N, DEPTH))
        py[0:3] = zeros((3, N, DEPTH))
        py[3:5] = zeros((2, N, DEPTH)) + 1.0

    @pl.when(gy == 1)
    def _():
        yb[0:N] = zeros((N, DEPTH))

    @pl.when(gy == ngy - 1)
    def _():
        yb[49 * N : 73 * N] = zeros((24 * N, DEPTH))
        xr[2 * N : 3 * N] = zeros((N, DEPTH))
        fy[...] = zeros((3, N, DEPTH))

    left_z = lax.broadcasted_iota(jnp.int32, (DEPTH, DEPTH), 0)
    right_z = lax.broadcasted_iota(jnp.int32, (DEPTH, DEPTH), 1)
    band_z = band(right_z - left_z) / coverage(right_z, DEPTH)
    place = lax.broadcasted_iota(jnp.int32, (25, CH, DEPTH), 0) - 1
    ix[...] = 1.0 / coverage(gx * N + place, ngx * N)
    iy[...] = 1.0 / coverage(gy * N + place, ngy * N)

    def along_z(block):
        shape = block.shape
        flat = block.reshape(-1, DEPTH)
        return jnp.dot(flat, band_z, precision=HIGHEST, preferred_element_type=F32).reshape(shape)

    def gradients(i, y0, y1):
        lane = lax.broadcasted_iota(jnp.int32, (y1 - y0, DEPTH), 1)
        centre = [de[j, i, y0:y1, :] for j in range(3)]
        ahead = [
            [de[j, i + 1, y0:y1, :] for j in range(3)],
            [de[j, i, y0 + 1 : y1 + 1, :] for j in range(3)],
            [jnp.where(lane < DEPTH - 1, pltpu.roll(centre[j], DEPTH - 1, 1), 0.0) for j in range(3)],
        ]
        return [[ahead[a][j] - centre[j] for j in range(3)] for a in range(3)]

    def equivalent(i, y0, y1):
        g = gradients(i, y0, y1)
        xy, xz, yz = g[0][1] + g[1][0], g[0][2] + g[2][0], g[1][2] + g[2][1]
        squares = g[0][0] * g[0][0] + g[1][1] * g[1][1] + g[2][2] * g[2][2]
        squares = squares + 0.5 * (xy * xy + xz * xz + yz * yz)
        er[i, y0:y1, :] = jnp.sqrt(squares)

    local[0].wait()
    for j in range(3):
        fys[j] = de[j, 0:N, 0, :]

    def early(i, carry):
        equivalent(i, 0, 16)
        return carry

    lax.fori_loop(0, N - 1, early, 0)
    e[pl.ds(25, 23), 0:16, :] = along_z(er[pl.ds(0, 23), 0:16, :])

    pl.semaphore_wait(barrier, partners)
    start(front_x)
    start(front_y)
    for c in range(2):
        for k in part_x[c]:
            start(k)

    local[1].wait()
    local[2].wait()

    def material(i, carry):
        zz = z[i]
        bits = [(zz & 1) != 0, (zz & 2) != 0, (zz & 4) != 0]
        tm[i] = lookup(bits, threshold)
        rm[i] = 0.1 / lookup(bits, density)
        u[5, i] = lookup(bits, modulus)
        return carry

    lax.fori_loop(0, N, material, 0)

    arrived(front_x)
    arrived(front_y)
    for j in range(3):
        de[j, 0:N, N, :] = fy[j]

    def late(i, carry):
        equivalent(i, 16, 24)
        return carry

    lax.fori_loop(0, N - 1, late, 0)
    equivalent(N - 1, 0, N)
    e[48] = along_z(er[N - 1])
    for k in last_x:
        start(k)
    e[pl.ds(25, 23), 16:24, :] = along_z(er[pl.ds(0, 23), 16:24, :])
    for k in part_x[2]:
        start(k)

    def undamaged(i, carry):
        g = gradients(i, 0, N)
        mu = u[5, i]
        trace = mu * (g[0][0] + g[1][1] + g[2][2])
        xy, yy, yz = mu * (g[0][1] + g[1][0]), trace + 2.0 * mu * g[1][1], mu * (g[1][2] + g[2][1])
        u[0, i] = trace + 2.0 * mu * g[0][0]
        u[1, i] = xy
        u[2, i] = mu * (g[0][2] + g[2][0])
        u[3, i] = yy
        u[4, i] = yz
        u[5, i] = trace + 2.0 * mu * g[2][2]
        return carry

    lax.fori_loop(0, N, undamaged, 0)
    for k, source in enumerate((u.at[0], u.at[1], u.at[2], h, tm)):
        pxs[k] = source[N - 1]
    for k, source in enumerate((u.at[1], u.at[3], u.at[4], h, tm)):
        pys[k] = source[0:N, N - 1, :]
    start(face_x)
    start(face_y)

    for c in range(3):
        for k in part_x[c]:
            arrived(k)
        if c == 0:
            for k in last_x:
                arrived(k)
        span = slice(c * CH, (c + 1) * CH)
        middle = taps(lambda t: e[t : t + 25, span, :]) * ix[...]
        xr[N + c * CH : N + (c + 1) * CH, :] = middle[0]
        for i in range(N):
            yb[pl.ds((25 + c * CH) * N + i, CH, stride=N), :] = middle[i + 1]
        for k in part_y[c]:
            start(k)
    for k in edge_y:
        start(k)

    for c in range(3):
        for k in part_y[c]:
            arrived(k)
    for k in edge_y:
        arrived(k)

    def across(g, carry):
        off = pl.multiple_of(g * CH, CH)
        read = lambda t: jnp.stack([yb[pl.ds((m + t) * N + off, CH), :] for m in range(25)])
        total = taps(read) * iy[...]
        for m in range(25):
            out[pl.ds(m * N + off, CH), :] = total[m]
        return carry

    lax.fori_loop(0, N // CH, across, 0)

    arrived(face_x)
    arrived(face_y)

    def intact(history, average, limit):
        bounded = jnp.maximum(jnp.maximum(history, average), limit)
        return limit / bounded * jnp.exp(-0.5 * (bounded - limit))

    row = lax.broadcasted_iota(jnp.int32, (N, 3 * N), 0)
    col = lax.broadcasted_iota(jnp.int32, (N, 3 * N), 1)
    weights = band(col - N - row) / coverage(gy * N + row, ngy * N)
    average_x = jnp.dot(weights, xr[...], precision=HIGHEST, preferred_element_type=F32)
    whole_x = intact(px[3], average_x, px[4])
    whole_y = intact(py[3], out[0:N, :], py[4])
    for j in range(3):
        pyi[j] = whole_y * py[j]

    local[3].wait()
    lane = lax.broadcasted_iota(jnp.int32, (N, DEPTH), 1)
    sub = lax.broadcasted_iota(jnp.int32, (N, DEPTH), 0)

    def finish(i, before):
        average = out[pl.ds(N + i, N, stride=N), :]
        top = jnp.maximum(h[i], average)
        nh[i] = top
        limit = tm[i]
        bounded = jnp.maximum(top, limit)
        whole = limit / bounded * jnp.exp(-0.5 * (bounded - limit))
        s = [whole * u[k, i] for k in range(6)]
        sx, sy, sz = (s[0], s[1], s[2]), (s[1], s[3], s[4]), (s[2], s[4], s[5])
        rate = rm[i]
        for j in range(3):
            back_y = jnp.where(sub > 0, pltpu.roll(sy[j], 1, 0), pyi[j, pl.ds(i, 1), :])
            back_z = jnp.where(lane > 0, pltpu.roll(sz[j], 1, 1), 0.0)
            force = sx[j] - before[j] + (sy[j] - back_y) + (sz[j] - back_z)
            speed = v[j, i] + rate * force
            nv[j, i] = speed
            nd[j, i] = de[j, i, 0:N, :] + 0.1 * speed
        return sx

    lax.fori_loop(0, N, finish, tuple(whole_x * px[j] for j in range(3)))

    done = [
        pltpu.make_async_copy(nd, nd_out, lsem.at[0]),
        pltpu.make_async_copy(nv, nv_out, lsem.at[1]),
        pltpu.make_async_copy(nh, nh_out, lsem.at[2]),
    ]
    for copy in done:
        copy.start()
    for k in range(len(made)):
        left(k)
    for copy in done:
        copy.wait()


COPIES = 22


def body(ngx, ngy, displacement, velocity, history, zone, zone_modulus, zone_threshold, zone_density):
    block = (N, N, DEPTH)
    plane = (N, DEPTH)
    anywhere = pl.BlockSpec(memory_space=pl.ANY)
    table = pl.BlockSpec(memory_space=pltpu.SMEM)
    vmem = lambda *shape: pltpu.VMEM(shape, F32)
    return pl.pallas_call(
        functools.partial(kernel, ngx, ngy),
        out_shape=(
            jax.ShapeDtypeStruct((3, *block), F32),
            jax.ShapeDtypeStruct((3, *block), F32),
            jax.ShapeDtypeStruct(block, F32),
        ),
        in_specs=[anywhere] * 4 + [table] * 3,
        out_specs=(anywhere, anywhere, anywhere),
        scratch_shapes=[
            vmem(3, N + 1, 32, DEPTH),
            vmem(3, *block),
            vmem(*block),
            pltpu.VMEM(block, jnp.int32),
            vmem(3, *plane),
            vmem(3, *plane),
            vmem(*block),
            vmem(73, *plane),
            vmem(73 * N, DEPTH),
            vmem(25 * N, DEPTH),
            vmem(3 * N, DEPTH),
            vmem(6, *block),
            vmem(*block),
            vmem(*block),
            vmem(25, CH, DEPTH),
            vmem(25, CH, DEPTH),
            vmem(5, *plane),
            vmem(5, *plane),
            vmem(5, *plane),
            vmem(5, *plane),
            vmem(3, *plane),
            vmem(3, *block),
            vmem(3, *block),
            vmem(*block),
            pltpu.SemaphoreType.DMA((4,)),
            pltpu.SemaphoreType.DMA((COPIES,)),
            pltpu.SemaphoreType.DMA((COPIES,)),
        ],
        compiler_params=pltpu.CompilerParams(
            collective_id=0, has_side_effects=True, vmem_limit_bytes=40 * 1024 * 1024
        ),
    )(displacement, velocity, history, zone, zone_modulus, zone_threshold, zone_density)


def solution(mesh):
    return jax.shard_map(
        functools.partial(body, mesh.shape["gx"], mesh.shape["gy"]),
        mesh=mesh,
        in_specs=(
            P(None, "gx", "gy", None),
            P(None, "gx", "gy", None),
            P("gx", "gy", None),
            P("gx", "gy", None),
            P(),
            P(),
            P(),
        ),
        out_specs=(P(None, "gx", "gy", None), P(None, "gx", "gy", None), P("gx", "gy", None)),
        check_vma=False,
    )
```

```python
import functools

import jax
import jax.numpy as jnp
from jax import lax
from jax.experimental import pallas as pl
from jax.experimental.pallas import tpu as pltpu
from jax.sharding import PartitionSpec as P

RADIUS = 24
TAPS = 2 * RADIUS + 1
N = 24
DEPTH = 128
CH = 8
F32 = jnp.float32
MESH = pl.DeviceIdType.MESH
HIGHEST = lax.Precision.HIGHEST

WEIGHT = [1.0 - 0.5 * ((t - RADIUS) / RADIUS) ** 2 for t in range(TAPS)]


def ramp(a):
    return (a * (a + 1) * (2 * a + 1)).astype(F32) * (1.0 / 6.0)


def coverage(place, total):
    low = jnp.minimum(place, RADIUS)
    high = jnp.minimum(total - 1 - place, RADIUS)
    return (low + high + 1).astype(F32) - (ramp(low) + ramp(high)) * (0.5 / RADIUS**2)


def band(offset):
    ratio = offset.astype(F32) * (1.0 / RADIUS)
    return jnp.where(jnp.abs(offset) <= RADIUS, 1.0 - 0.5 * ratio * ratio, 0.0)


def lookup(bits, table):
    level = [table[k] for k in range(8)]
    for bit in bits:
        level = [jnp.where(bit, level[k + 1], level[k]) for k in range(0, len(level), 2)]
    return level[0]


def taps(rows):
    total = rows(RADIUS)
    for t in range(RADIUS):
        total = total + WEIGHT[t] * (rows(t) + rows(TAPS - 1 - t))
    return total


def kernel(
    ngx, ngy,
    disp, vel, hist, zone, modulus_in, threshold_in, density_in,
    nd, nv, nh,
    de, v, h, z, fys, fy, er, e, yb, out, xr, u, tm, rm, ix, iy, pxs, px, pys, py, pyi,
    modulus, threshold, density, lsem, ssem, rsem,
):
    gx = lax.axis_index("gx")
    gy = lax.axis_index("gy")
    where_am = {"gx": gx, "gy": gy}
    count = {"gx": ngx, "gy": ngy}

    def reach(axis, step):
        place = where_am[axis] + step
        return (place >= 0) & (place < count[axis])

    local = [
        pltpu.make_async_copy(disp, de.at[:, pl.ds(0, N), pl.ds(0, N), :], lsem.at[0]),
        pltpu.make_async_copy(hist, h, lsem.at[1]),
        pltpu.make_async_copy(zone, z, lsem.at[2]),
        pltpu.make_async_copy(vel, v, lsem.at[3]),
        pltpu.make_async_copy(modulus_in, modulus, lsem.at[4]),
        pltpu.make_async_copy(threshold_in, threshold, lsem.at[5]),
        pltpu.make_async_copy(density_in, density, lsem.at[6]),
    ]
    for copy in local:
        copy.start()

    barrier = pltpu.get_barrier_semaphore()
    partners = jnp.int32(0)
    for axis in ("gx", "gy"):
        for step in (-2, -1, 1, 2):
            ok = reach(axis, step)
            partners = partners + jnp.where(ok, 1, 0)

            @pl.when(ok)
            def _(axis=axis, step=step):
                pl.semaphore_signal(
                    barrier, inc=1, device_id={axis: where_am[axis] + step}, device_id_type=MESH
                )

    made = []

    def remote(src, dst, axis, step):
        k = len(made)
        copy = pltpu.make_async_remote_copy(
            src_ref=src,
            dst_ref=dst,
            send_sem=ssem.at[k],
            recv_sem=rsem.at[k],
            device_id={axis: where_am[axis] + step},
            device_id_type=MESH,
        )
        made.append((copy, axis, step))
        return k

    def start(k):
        copy, axis, step = made[k]
        pl.when(reach(axis, step))(copy.start)

    def arrived(k):
        copy, axis, step = made[k]
        pl.when(reach(axis, -step))(copy.wait_recv)

    def left(k):
        copy, axis, step = made[k]
        pl.when(reach(axis, step))(copy.wait_send)

    def rows(ref, first, number):
        return ref.at[pl.ds(first * N, number * N), :]

    front_x = remote(de.at[:, 0, pl.ds(0, N), :], de.at[:, N, pl.ds(0, N), :], "gx", -1)
    front_y = remote(fys, fy, "gy", -1)
    part_x = []
    for c in range(3):
        span = pl.ds(c * CH, CH)
        src = e.at[pl.ds(25, 23), span, :]
        part_x.append(
            (
                remote(src, e.at[pl.ds(1, 23), span, :], "gx", 1),
                remote(src, e.at[pl.ds(49, 23), span, :], "gx", -1),
            )
        )
    last_x = (
        remote(e.at[48], e.at[24], "gx", 1),
        remote(e.at[48], e.at[72], "gx", -1),
        remote(e.at[48], e.at[0], "gx", 2),
    )
    part_y = []
    for c in range(3):
        src = rows(yb, 25 + c * CH, CH)
        part_y.append(
            (
                remote(src, rows(yb, 1 + c * CH, CH), "gy", 1),
                remote(src, rows(yb, 49 + c * CH, CH), "gy", -1),
            )
        )
    edge_y = (
        remote(rows(yb, 48, 1), rows(yb, 0, 1), "gy", 2),
        remote(xr.at[pl.ds(N, N), :], xr.at[pl.ds(0, N), :], "gy", 1),
        remote(xr.at[pl.ds(N, N), :], xr.at[pl.ds(2 * N, N), :], "gy", -1),
    )
    face_x = remote(pxs, px, "gx", 1)
    face_y = remote(pys, py, "gy", 1)

    zeros = functools.partial(jnp.zeros, dtype=F32)

    @pl.when(gx == 0)
    def _():
        e[pl.ds(0, 25)] = zeros((25, N, DEPTH))
        px[0:3] = zeros((3, N, DEPTH))
        px[3:5] = zeros((2, N, DEPTH)) + 1.0

    @pl.when(gx == 1)
    def _():
        e[0] = zeros((N, DEPTH))

    @pl.when(gx == ngx - 1)
    def _():
        e[pl.ds(49, 24)] = zeros((24, N, DEPTH))
        for j in range(3):
            de[j, N, 0:N, :] = zeros((N, DEPTH))

    @pl.when(gy == 0)
    def _():
        yb[0 : 25 * N] = zeros((25 * N, DEPTH))
        xr[0:N] = zeros((N, DEPTH))
        py[0:3] = zeros((3, N, DEPTH))
        py[3:5] = zeros((2, N, DEPTH)) + 1.0

    @pl.when(gy == 1)
    def _():
        yb[0:N] = zeros((N, DEPTH))

    @pl.when(gy == ngy - 1)
    def _():
        yb[49 * N : 73 * N] = zeros((24 * N, DEPTH))
        xr[2 * N : 3 * N] = zeros((N, DEPTH))
        fy[...] = zeros((3, N, DEPTH))

    left_z = lax.broadcasted_iota(jnp.int32, (DEPTH, DEPTH), 0)
    right_z = lax.broadcasted_iota(jnp.int32, (DEPTH, DEPTH), 1)
    band_z = band(right_z - left_z) / coverage(right_z, DEPTH)
    place = lax.broadcasted_iota(jnp.int32, (25, CH, DEPTH), 0) - 1
    ix[...] = 1.0 / coverage(gx * N + place, ngx * N)
    iy[...] = 1.0 / coverage(gy * N + place, ngy * N)

    def along_z(block):
        shape = block.shape
        flat = block.reshape(-1, DEPTH)
        return jnp.dot(flat, band_z, precision=HIGHEST, preferred_element_type=F32).reshape(shape)

    def gradients(i, y0, y1):
        lane = lax.broadcasted_iota(jnp.int32, (y1 - y0, DEPTH), 1)
        centre = [de[j, i, y0:y1, :] for j in range(3)]
        ahead = [
            [de[j, i + 1, y0:y1, :] for j in range(3)],
            [de[j, i, y0 + 1 : y1 + 1, :] for j in range(3)],
            [jnp.where(lane < DEPTH - 1, pltpu.roll(centre[j], DEPTH - 1, 1), 0.0) for j in range(3)],
        ]
        return [[ahead[a][j] - centre[j] for j in range(3)] for a in range(3)]

    def equivalent(i, y0, y1):
        g = gradients(i, y0, y1)
        xy, xz, yz = g[0][1] + g[1][0], g[0][2] + g[2][0], g[1][2] + g[2][1]
        squares = g[0][0] * g[0][0] + g[1][1] * g[1][1] + g[2][2] * g[2][2]
        squares = squares + 0.5 * (xy * xy + xz * xz + yz * yz)
        er[i, y0:y1, :] = jnp.sqrt(squares)

    local[0].wait()
    for j in range(3):
        fys[j] = de[j, 0:N, 0, :]

    def early(i, carry):
        equivalent(i, 0, 16)
        return carry

    lax.fori_loop(0, N - 1, early, 0, unroll=True)
    e[pl.ds(25, 23), 0:16, :] = along_z(er[pl.ds(0, 23), 0:16, :])

    pl.semaphore_wait(barrier, partners)
    start(front_x)
    start(front_y)
    for c in range(2):
        for k in part_x[c]:
            start(k)

    for k in (1, 2, 4, 5, 6):
        local[k].wait()

    def material(i, carry):
        zz = z[i]
        bits = [(zz & 1) != 0, (zz & 2) != 0, (zz & 4) != 0]
        tm[i] = lookup(bits, threshold)
        rm[i] = 0.1 / lookup(bits, density)
        u[5, i] = lookup(bits, modulus)
        return carry

    lax.fori_loop(0, N, material, 0, unroll=4)

    arrived(front_x)
    arrived(front_y)
    for j in range(3):
        de[j, 0:N, N, :] = fy[j]

    def late(i, carry):
        equivalent(i, 16, 24)
        return carry

    lax.fori_loop(0, N - 1, late, 0, unroll=True)
    equivalent(N - 1, 0, N)
    e[48] = along_z(er[N - 1])
    for k in last_x:
        start(k)
    e[pl.ds(25, 23), 16:24, :] = along_z(er[pl.ds(0, 23), 16:24, :])
    for k in part_x[2]:
        start(k)

    def undamaged(i, carry):
        g = gradients(i, 0, N)
        mu = u[5, i]
        trace = mu * (g[0][0] + g[1][1] + g[2][2])
        xy, yy, yz = mu * (g[0][1] + g[1][0]), trace + 2.0 * mu * g[1][1], mu * (g[1][2] + g[2][1])
        u[0, i] = trace + 2.0 * mu * g[0][0]
        u[1, i] = xy
        u[2, i] = mu * (g[0][2] + g[2][0])
        u[3, i] = yy
        u[4, i] = yz
        u[5, i] = trace + 2.0 * mu * g[2][2]
        return carry

    lax.fori_loop(0, N, undamaged, 0, unroll=4)
    for k, source in enumerate((u.at[0], u.at[1], u.at[2], h, tm)):
        pxs[k] = source[N - 1]
    for k, source in enumerate((u.at[1], u.at[3], u.at[4], h, tm)):
        pys[k] = source[0:N, N - 1, :]
    start(face_x)
    start(face_y)

    for c in range(3):
        for k in part_x[c]:
            arrived(k)
        if c == 0:
            for k in last_x:
                arrived(k)
        span = slice(c * CH, (c + 1) * CH)
        middle = taps(lambda t: e[t : t + 25, span, :]) * ix[...]
        xr[N + c * CH : N + (c + 1) * CH, :] = middle[0]
        for i in range(N):
            yb[pl.ds((25 + c * CH) * N + i, CH, stride=N), :] = middle[i + 1]
        for k in part_y[c]:
            start(k)
    for k in edge_y:
        start(k)

    for c in range(3):
        for k in part_y[c]:
            arrived(k)
    for k in edge_y:
        arrived(k)

    def across(g, carry):
        off = pl.multiple_of(g * CH, CH)
        read = lambda t: jnp.stack([yb[pl.ds((m + t) * N + off, CH), :] for m in range(25)])
        total = taps(read) * iy[...]
        for m in range(25):
            out[pl.ds(m * N + off, CH), :] = total[m]
        return carry

    lax.fori_loop(0, N // CH, across, 0)

    arrived(face_x)
    arrived(face_y)

    def intact(history, average, limit):
        bounded = jnp.maximum(jnp.maximum(history, average), limit)
        return limit / bounded * jnp.exp(-0.5 * (bounded - limit))

    row = lax.broadcasted_iota(jnp.int32, (N, 3 * N), 0)
    col = lax.broadcasted_iota(jnp.int32, (N, 3 * N), 1)
    weights = band(col - N - row) / coverage(gy * N + row, ngy * N)
    average_x = jnp.dot(weights, xr[...], precision=HIGHEST, preferred_element_type=F32)
    whole_x = intact(px[3], average_x, px[4])
    whole_y = intact(py[3], out[0:N, :], py[4])
    for j in range(3):
        pyi[j] = whole_y * py[j]

    local[3].wait()
    lane = lax.broadcasted_iota(jnp.int32, (N, DEPTH), 1)
    sub = lax.broadcasted_iota(jnp.int32, (N, DEPTH), 0)

    def finish(i, before):
        average = out[pl.ds(N + i, N, stride=N), :]
        top = jnp.maximum(h[i], average)
        nh[i] = top
        limit = tm[i]
        bounded = jnp.maximum(top, limit)
        whole = limit / bounded * jnp.exp(-0.5 * (bounded - limit))
        s = [whole * u[k, i] for k in range(6)]
        sx, sy, sz = (s[0], s[1], s[2]), (s[1], s[3], s[4]), (s[2], s[4], s[5])
        rate = rm[i]
        for j in range(3):
            back_y = jnp.where(sub > 0, pltpu.roll(sy[j], 1, 0), pyi[j, pl.ds(i, 1), :])
            back_z = jnp.where(lane > 0, pltpu.roll(sz[j], 1, 1), 0.0)
            force = sx[j] - before[j] + (sy[j] - back_y) + (sz[j] - back_z)
            speed = v[j, i] + rate * force
            nv[j, i] = speed
            nd[j, i] = de[j, i, 0:N, :] + 0.1 * speed
        return sx

    lax.fori_loop(0, N, finish, tuple(whole_x * px[j] for j in range(3)), unroll=4)

    for k in range(len(made)):
        left(k)


def store(nd, nv, nh, nd_out, nv_out, nh_out, sem):
    done = [
        pltpu.make_async_copy(source, target, sem.at[k])
        for k, (source, target) in enumerate(((nd, nd_out), (nv, nv_out), (nh, nh_out)))
    ]
    for copy in done:
        copy.start()
    for copy in done:
        copy.wait()


COPIES = 22


def body(ngx, ngy, displacement, velocity, history, zone, zone_modulus, zone_threshold, zone_density):
    block = (N, N, DEPTH)
    plane = (N, DEPTH)
    whole = pl.BlockSpec(memory_space=pltpu.VMEM)
    fixed = pl.BlockSpec(memory_space=pltpu.HBM)
    vmem = lambda *shape: pltpu.VMEM(shape, F32)
    hold = lambda array: pltpu.with_memory_space_constraint(array, pltpu.HBM)
    results = pl.pallas_call(
        functools.partial(kernel, ngx, ngy),
        out_shape=(vmem(3, *block), vmem(3, *block), vmem(*block)),
        in_specs=[fixed] * 7,
        out_specs=(whole, whole, whole),
        scratch_shapes=[
            vmem(3, N + 1, 32, DEPTH),
            vmem(3, *block),
            vmem(*block),
            pltpu.VMEM(block, jnp.int32),
            vmem(3, *plane),
            vmem(3, *plane),
            vmem(*block),
            vmem(73, *plane),
            vmem(73 * N, DEPTH),
            vmem(25 * N, DEPTH),
            vmem(3 * N, DEPTH),
            vmem(6, *block),
            vmem(*block),
            vmem(*block),
            vmem(25, CH, DEPTH),
            vmem(25, CH, DEPTH),
            vmem(5, *plane),
            vmem(5, *plane),
            vmem(5, *plane),
            vmem(5, *plane),
            vmem(3, *plane),
            pltpu.SMEM((8,), F32),
            pltpu.SMEM((8,), F32),
            pltpu.SMEM((8,), F32),
            pltpu.SemaphoreType.DMA((7,)),
            pltpu.SemaphoreType.DMA((COPIES,)),
            pltpu.SemaphoreType.DMA((COPIES,)),
        ],
        compiler_params=pltpu.CompilerParams(
            collective_id=0, has_side_effects=True, vmem_limit_bytes=40 * 1024 * 1024
        ),
    )(*(hold(a) for a in (displacement, velocity, history, zone, zone_modulus, zone_threshold, zone_density)))
    return pl.pallas_call(
        store,
        out_shape=tuple(jax.ShapeDtypeStruct(r.shape, F32) for r in results),
        in_specs=[whole] * 3,
        out_specs=(fixed,) * 3,
        scratch_shapes=[pltpu.SemaphoreType.DMA((3,))],
    )(*(pltpu.with_memory_space_constraint(r, pltpu.VMEM) for r in results))


def solution(mesh):
    return jax.shard_map(
        functools.partial(body, mesh.shape["gx"], mesh.shape["gy"]),
        mesh=mesh,
        in_specs=(
            P(None, "gx", "gy", None),
            P(None, "gx", "gy", None),
            P("gx", "gy", None),
            P("gx", "gy", None),
            P(),
            P(),
            P(),
        ),
        out_specs=(P(None, "gx", "gy", None), P(None, "gx", "gy", None), P("gx", "gy", None)),
        check_vma=False,
    )
```

```python
import functools

import jax
import jax.numpy as jnp
from jax import lax
from jax.experimental import pallas as pl
from jax.experimental.pallas import tpu as pltpu
from jax.sharding import PartitionSpec as P

RADIUS = 24
TAPS = 2 * RADIUS + 1
N = 24
DEPTH = 128
CH = 8
F32 = jnp.float32
MESH = pl.DeviceIdType.MESH
HIGHEST = lax.Precision.HIGHEST

WEIGHT = [1.0 - 0.5 * ((t - RADIUS) / RADIUS) ** 2 for t in range(TAPS)]


def ramp(a):
    return (a * (a + 1) * (2 * a + 1)).astype(F32) * (1.0 / 6.0)


def coverage(place, total):
    low = jnp.minimum(place, RADIUS)
    high = jnp.minimum(total - 1 - place, RADIUS)
    return (low + high + 1).astype(F32) - (ramp(low) + ramp(high)) * (0.5 / RADIUS**2)


def band(offset):
    ratio = offset.astype(F32) * (1.0 / RADIUS)
    return jnp.where(jnp.abs(offset) <= RADIUS, 1.0 - 0.5 * ratio * ratio, 0.0)


def lookup(bits, table):
    level = [table[k] for k in range(8)]
    for bit in bits:
        level = [jnp.where(bit, level[k + 1], level[k]) for k in range(0, len(level), 2)]
    return level[0]


def taps(rows):
    total = rows(RADIUS)
    for t in range(RADIUS):
        total = total + WEIGHT[t] * (rows(t) + rows(TAPS - 1 - t))
    return total


def kernel(
    ngx, ngy,
    disp, vel, hist, zone, modulus_in, threshold_in, density_in,
    nd, nv, nh,
    de, v, h, z, fys, fy, er, e, yb, out, xr, u, tm, rm, ix, iy, ie, pxs, px, pys, py, pyi,
    modulus, threshold, density, lsem, ssem, rsem,
):
    gx = lax.axis_index("gx")
    gy = lax.axis_index("gy")
    where_am = {"gx": gx, "gy": gy}
    count = {"gx": ngx, "gy": ngy}

    def reach(axis, step):
        place = where_am[axis] + step
        return (place >= 0) & (place < count[axis])

    local = [
        pltpu.make_async_copy(disp, de.at[:, pl.ds(0, N), pl.ds(0, N), :], lsem.at[0]),
        pltpu.make_async_copy(hist, h, lsem.at[1]),
        pltpu.make_async_copy(zone, z, lsem.at[2]),
        pltpu.make_async_copy(vel, v, lsem.at[3]),
        pltpu.make_async_copy(modulus_in, modulus, lsem.at[4]),
        pltpu.make_async_copy(threshold_in, threshold, lsem.at[5]),
        pltpu.make_async_copy(density_in, density, lsem.at[6]),
    ]
    for copy in local:
        copy.start()

    barrier = pltpu.get_barrier_semaphore()
    partners = jnp.int32(0)
    for axis in ("gx", "gy"):
        for step in (-1, 1):
            ok = reach(axis, step)
            partners = partners + jnp.where(ok, 1, 0)

            @pl.when(ok)
            def _(axis=axis, step=step):
                pl.semaphore_signal(
                    barrier, inc=1, device_id={axis: where_am[axis] + step}, device_id_type=MESH
                )

    made = []

    def remote(src, dst, axis, step):
        k = len(made)
        copy = pltpu.make_async_remote_copy(
            src_ref=src,
            dst_ref=dst,
            send_sem=ssem.at[k],
            recv_sem=rsem.at[k],
            device_id={axis: where_am[axis] + step},
            device_id_type=MESH,
        )
        made.append((copy, axis, step))
        return k

    def start(k):
        copy, axis, step = made[k]
        pl.when(reach(axis, step))(copy.start)

    def far(step):
        return lax.rem(gx, 4) == (3 if step > 0 else 0)

    def start_far(k):
        copy, axis, step = made[k]
        pl.when(reach(axis, step) & far(step))(copy.start)

    def start_near(k):
        copy, axis, step = made[k]
        pl.when(reach(axis, step) & jnp.logical_not(far(step)))(copy.start)

    def arrived(k):
        copy, axis, step = made[k]
        pl.when(reach(axis, -step))(copy.wait_recv)

    def left(k):
        copy, axis, step = made[k]
        pl.when(reach(axis, step))(copy.wait_send)

    def rows(ref, first, number):
        return ref.at[pl.ds(first * N, number * N), :]

    front_x = remote(de.at[:, 0, pl.ds(0, N), :], de.at[:, N, pl.ds(0, N), :], "gx", -1)
    front_y = remote(fys, fy, "gy", -1)
    part_x = []
    for c in range(3):
        src = e.at[c, pl.ds(25, 23)]
        part_x.append(
            (
                remote(src, e.at[c, pl.ds(1, 23)], "gx", 1),
                remote(src, e.at[c, pl.ds(49, 23)], "gx", -1),
            )
        )
    last_x = (
        remote(e.at[:, 48], e.at[:, 24], "gx", 1),
        remote(e.at[:, 48], e.at[:, 72], "gx", -1),
        remote(e.at[:, 48], e.at[:, 0], "gx", 2),
    )
    part_y = []
    for c in range(3):
        src = rows(yb, 25 + c * CH, CH)
        part_y.append(
            (
                remote(src, rows(yb, 1 + c * CH, CH), "gy", 1),
                remote(src, rows(yb, 49 + c * CH, CH), "gy", -1),
            )
        )
    edge_y = (
        remote(rows(yb, 48, 1), rows(yb, 0, 1), "gy", 2),
        remote(xr.at[pl.ds(N, N), :], xr.at[pl.ds(0, N), :], "gy", 1),
        remote(xr.at[pl.ds(N, N), :], xr.at[pl.ds(2 * N, N), :], "gy", -1),
    )
    face_x = remote(pxs, px, "gx", 1)
    face_y = remote(pys, py, "gy", 1)

    zeros = functools.partial(jnp.zeros, dtype=F32)

    @pl.when(gx == 0)
    def _():
        e[:, 0:25] = zeros((3, 25, CH, DEPTH))
        px[0:3] = zeros((3, N, DEPTH))
        px[3:5] = zeros((2, N, DEPTH)) + 1.0

    @pl.when(gx == 1)
    def _():
        e[:, 0] = zeros((3, CH, DEPTH))

    @pl.when(gx == ngx - 1)
    def _():
        e[:, 49:73] = zeros((3, 24, CH, DEPTH))
        for j in range(3):
            de[j, N, 0:N, :] = zeros((N, DEPTH))

    @pl.when(gy == 0)
    def _():
        yb[0 : 25 * N] = zeros((25 * N, DEPTH))
        xr[0:N] = zeros((N, DEPTH))
        py[0:3] = zeros((3, N, DEPTH))
        py[3:5] = zeros((2, N, DEPTH)) + 1.0

    @pl.when(gy == 1)
    def _():
        yb[0:N] = zeros((N, DEPTH))

    @pl.when(gy == ngy - 1)
    def _():
        yb[49 * N : 73 * N] = zeros((24 * N, DEPTH))
        xr[2 * N : 3 * N] = zeros((N, DEPTH))
        fy[...] = zeros((3, N, DEPTH))

    left_z = lax.broadcasted_iota(jnp.int32, (DEPTH, DEPTH), 0)
    right_z = lax.broadcasted_iota(jnp.int32, (DEPTH, DEPTH), 1)
    band_z = band(right_z - left_z) / coverage(right_z, DEPTH)
    place = lax.broadcasted_iota(jnp.int32, (25, CH, DEPTH), 0) - 1
    ix[...] = 1.0 / coverage(gx * N + place, ngx * N)
    place = lax.broadcasted_iota(jnp.int32, (N, DEPTH), 0)
    iy[...] = 1.0 / coverage(gy * N + place, ngy * N)
    edge = lax.broadcasted_iota(jnp.int32, (CH, DEPTH), 0) - 1
    ie[...] = 1.0 / coverage(gy * N + edge, ngy * N)

    def along_z(block):
        shape = block.shape
        flat = block.reshape(-1, DEPTH)
        return jnp.dot(flat, band_z, precision=HIGHEST, preferred_element_type=F32).reshape(shape)

    def gradients(i, y0, y1):
        lane = lax.broadcasted_iota(jnp.int32, (y1 - y0, DEPTH), 1)
        centre = [de[j, i, y0:y1, :] for j in range(3)]
        ahead = [
            [de[j, i + 1, y0:y1, :] for j in range(3)],
            [de[j, i, y0 + 1 : y1 + 1, :] for j in range(3)],
            [jnp.where(lane < DEPTH - 1, pltpu.roll(centre[j], DEPTH - 1, 1), 0.0) for j in range(3)],
        ]
        return [[ahead[a][j] - centre[j] for j in range(3)] for a in range(3)]

    def equivalent(i, y0, y1):
        g = gradients(i, y0, y1)
        xy, xz, yz = g[0][1] + g[1][0], g[0][2] + g[2][0], g[1][2] + g[2][1]
        squares = g[0][0] * g[0][0] + g[1][1] * g[1][1] + g[2][2] * g[2][2]
        squares = squares + 0.5 * (xy * xy + xz * xz + yz * yz)
        root = jnp.sqrt(squares)
        for c in range(y0 // CH, y1 // CH):
            er[c, i] = root[c * CH - y0 : (c + 1) * CH - y0]

    local[0].wait()
    for j in range(3):
        fys[j] = de[j, 0:N, 0, :]

    def early(i, carry):
        equivalent(i, 0, 16)
        return carry

    lax.fori_loop(0, N - 1, early, 0, unroll=True)
    e[0:2, 25:48] = along_z(er[0:2, 0:23])

    pl.semaphore_wait(barrier, partners)
    start(front_x)
    start(front_y)
    for c in range(2):
        for k in part_x[c]:
            start_far(k)

    for k in (1, 2, 4, 5, 6):
        local[k].wait()

    def material(i, carry):
        zz = z[i]
        bits = [(zz & 1) != 0, (zz & 2) != 0, (zz & 4) != 0]
        tm[i] = lookup(bits, threshold)
        rm[i] = 0.1 / lookup(bits, density)
        u[5, i] = lookup(bits, modulus)
        return carry

    lax.fori_loop(0, N, material, 0, unroll=4)

    arrived(front_x)
    for k in part_x[0]:
        start_near(k)
    arrived(front_y)
    for j in range(3):
        de[j, 0:N, N, :] = fy[j]

    def late(i, carry):
        equivalent(i, 16, 24)
        return carry

    lax.fori_loop(0, N - 1, late, 0, unroll=True)
    equivalent(N - 1, 0, N)
    e[:, 48] = along_z(er[:, N - 1])
    for k in last_x:
        start(k)
    e[2, 25:48] = along_z(er[2, 0:23])
    for k in part_x[2]:
        start_far(k)
    for c in (1, 2):
        for k in part_x[c]:
            start_near(k)

    def undamaged(i, carry):
        g = gradients(i, 0, N)
        mu = u[5, i]
        trace = mu * (g[0][0] + g[1][1] + g[2][2])
        xy, yy, yz = mu * (g[0][1] + g[1][0]), trace + 2.0 * mu * g[1][1], mu * (g[1][2] + g[2][1])
        u[0, i] = trace + 2.0 * mu * g[0][0]
        u[1, i] = xy
        u[2, i] = mu * (g[0][2] + g[2][0])
        u[3, i] = yy
        u[4, i] = yz
        u[5, i] = trace + 2.0 * mu * g[2][2]
        return carry

    lax.fori_loop(0, N, undamaged, 0, unroll=4)
    for k, source in enumerate((u.at[0], u.at[1], u.at[2], h, tm)):
        pxs[k] = source[N - 1]
    for k, source in enumerate((u.at[1], u.at[3], u.at[4], h, tm)):
        pys[k] = source[0:N, N - 1, :]
    start(face_x)
    start(face_y)

    for c in range(3):
        for k in part_x[c]:
            arrived(k)
        if c == 0:
            for k in last_x:
                arrived(k)
        middle = taps(lambda t: e[c, t : t + 25]) * ix[...]
        xr[N + c * CH : N + (c + 1) * CH, :] = middle[0]
        for i in range(N):
            yb[pl.ds((25 + c * CH) * N + i, CH, stride=N), :] = middle[i + 1]
        for k in part_y[c]:
            start(k)
    for k in edge_y:
        start(k)

    def gather(first, number, fresh):
        def group(g, carry):
            off = pl.multiple_of(g * CH, CH)
            source = jnp.stack([yb[pl.ds((first + k) * N + off, CH), :] for k in range(number)])
            if fresh:
                total = jnp.zeros((25, CH, DEPTH), F32)
            else:
                total = jnp.stack([out[pl.ds(m * N + off, CH), :] for m in range(25)])
            for t in range(TAPS):
                lo, hi = max(0, first - t), min(25, first + number - t)
                if lo < hi:
                    part = total[lo:hi] + WEIGHT[t] * source[lo + t - first : hi + t - first]
                    pieces = [total[:lo]] * (lo > 0) + [part] + [total[hi:]] * (hi < 25)
                    total = jnp.concatenate(pieces) if len(pieces) > 1 else part
            for m in range(25):
                out[pl.ds(m * N + off, CH), :] = total[m]
            return carry

        lax.fori_loop(0, N // CH, group, 0)

    gather(25, N, True)
    for c in range(3):
        for k in part_y[c]:
            arrived(k)
        gather(1 + c * CH, CH, False)
        gather(49 + c * CH, CH, False)
    for k in edge_y:
        arrived(k)
    out[0:N] += WEIGHT[0] * yb[0:N]

    arrived(face_x)
    arrived(face_y)

    def intact(history, average, limit):
        bounded = jnp.maximum(jnp.maximum(history, average), limit)
        return limit / bounded * jnp.exp(-0.5 * (bounded - limit))

    row = lax.broadcasted_iota(jnp.int32, (N, 3 * N), 0)
    col = lax.broadcasted_iota(jnp.int32, (N, 3 * N), 1)
    weights = band(col - N - row) / coverage(gy * N + row, ngy * N)
    average_x = jnp.dot(weights, xr[...], precision=HIGHEST, preferred_element_type=F32)
    whole_x = intact(px[3], average_x, px[4])
    whole_y = intact(py[3], out[0:N, :] * ie[0:1, :], py[4])
    for j in range(3):
        pyi[j] = whole_y * py[j]

    local[3].wait()
    lane = lax.broadcasted_iota(jnp.int32, (N, DEPTH), 1)
    sub = lax.broadcasted_iota(jnp.int32, (N, DEPTH), 0)

    def finish(i, before):
        average = out[pl.ds(N + i, N, stride=N), :] * iy[...]
        top = jnp.maximum(h[i], average)
        nh[i] = top
        limit = tm[i]
        bounded = jnp.maximum(top, limit)
        whole = limit / bounded * jnp.exp(-0.5 * (bounded - limit))
        s = [whole * u[k, i] for k in range(6)]
        sx, sy, sz = (s[0], s[1], s[2]), (s[1], s[3], s[4]), (s[2], s[4], s[5])
        rate = rm[i]
        for j in range(3):
            back_y = jnp.where(sub > 0, pltpu.roll(sy[j], 1, 0), pyi[j, pl.ds(i, 1), :])
            back_z = jnp.where(lane > 0, pltpu.roll(sz[j], 1, 1), 0.0)
            force = sx[j] - before[j] + (sy[j] - back_y) + (sz[j] - back_z)
            speed = v[j, i] + rate * force
            nv[j, i] = speed
            nd[j, i] = de[j, i, 0:N, :] + 0.1 * speed
        return sx

    lax.fori_loop(0, N, finish, tuple(whole_x * px[j] for j in range(3)), unroll=4)

    for k in range(len(made)):
        left(k)


def store(nd, nv, nh, nd_out, nv_out, nh_out, sem):
    done = [
        pltpu.make_async_copy(source, target, sem.at[k])
        for k, (source, target) in enumerate(((nd, nd_out), (nv, nv_out), (nh, nh_out)))
    ]
    for copy in done:
        copy.start()
    for copy in done:
        copy.wait()


COPIES = 22


def body(ngx, ngy, displacement, velocity, history, zone, zone_modulus, zone_threshold, zone_density):
    block = (N, N, DEPTH)
    plane = (N, DEPTH)
    whole = pl.BlockSpec(memory_space=pltpu.VMEM)
    fixed = pl.BlockSpec(memory_space=pltpu.HBM)
    vmem = lambda *shape: pltpu.VMEM(shape, F32)
    hold = lambda array: pltpu.with_memory_space_constraint(array, pltpu.HBM)
    results = pl.pallas_call(
        functools.partial(kernel, ngx, ngy),
        out_shape=(vmem(3, *block), vmem(3, *block), vmem(*block)),
        in_specs=[fixed] * 7,
        out_specs=(whole, whole, whole),
        scratch_shapes=[
            vmem(3, N + 1, 32, DEPTH),
            vmem(3, *block),
            vmem(*block),
            pltpu.VMEM(block, jnp.int32),
            vmem(3, *plane),
            vmem(3, *plane),
            vmem(3, N, CH, DEPTH),
            vmem(3, 73, CH, DEPTH),
            vmem(73 * N, DEPTH),
            vmem(25 * N, DEPTH),
            vmem(3 * N, DEPTH),
            vmem(6, *block),
            vmem(*block),
            vmem(*block),
            vmem(25, CH, DEPTH),
            vmem(*plane),
            vmem(CH, DEPTH),
            vmem(5, *plane),
            vmem(5, *plane),
            vmem(5, *plane),
            vmem(5, *plane),
            vmem(3, *plane),
            pltpu.SMEM((8,), F32),
            pltpu.SMEM((8,), F32),
            pltpu.SMEM((8,), F32),
            pltpu.SemaphoreType.DMA((7,)),
            pltpu.SemaphoreType.DMA((COPIES,)),
            pltpu.SemaphoreType.DMA((COPIES,)),
        ],
        compiler_params=pltpu.CompilerParams(
            collective_id=0, has_side_effects=True, vmem_limit_bytes=40 * 1024 * 1024
        ),
    )(*(hold(a) for a in (displacement, velocity, history, zone, zone_modulus, zone_threshold, zone_density)))
    return pl.pallas_call(
        store,
        out_shape=tuple(jax.ShapeDtypeStruct(r.shape, F32) for r in results),
        in_specs=[whole] * 3,
        out_specs=(fixed,) * 3,
        scratch_shapes=[pltpu.SemaphoreType.DMA((3,))],
    )(*(pltpu.with_memory_space_constraint(r, pltpu.VMEM) for r in results))


def solution(mesh):
    return jax.shard_map(
        functools.partial(body, mesh.shape["gx"], mesh.shape["gy"]),
        mesh=mesh,
        in_specs=(
            P(None, "gx", "gy", None),
            P(None, "gx", "gy", None),
            P("gx", "gy", None),
            P("gx", "gy", None),
            P(),
            P(),
            P(),
        ),
        out_specs=(P(None, "gx", "gy", None), P(None, "gx", "gy", None), P("gx", "gy", None)),
        check_vma=False,
    )
```

```python
import functools

import jax
import jax.numpy as jnp
from jax import lax
from jax.experimental import pallas as pl
from jax.experimental.pallas import tpu as pltpu
from jax.sharding import PartitionSpec as P

RADIUS = 24
TAPS = 2 * RADIUS + 1
N = 24
DEPTH = 128
CH = 8
F32 = jnp.float32
MESH = pl.DeviceIdType.MESH
HIGHEST = lax.Precision.HIGHEST

WEIGHT = [1.0 - 0.5 * ((t - RADIUS) / RADIUS) ** 2 for t in range(TAPS)]


def ramp(a):
    return (a * (a + 1) * (2 * a + 1)).astype(F32) * (1.0 / 6.0)


def coverage(place, total):
    low = jnp.minimum(place, RADIUS)
    high = jnp.minimum(total - 1 - place, RADIUS)
    return (low + high + 1).astype(F32) - (ramp(low) + ramp(high)) * (0.5 / RADIUS**2)


def band(offset):
    ratio = offset.astype(F32) * (1.0 / RADIUS)
    return jnp.where(jnp.abs(offset) <= RADIUS, 1.0 - 0.5 * ratio * ratio, 0.0)


def lookup(bits, table):
    level = [table[k] for k in range(8)]
    for bit in bits:
        level = [jnp.where(bit, level[k + 1], level[k]) for k in range(0, len(level), 2)]
    return level[0]


def taps(rows):
    total = rows(RADIUS)
    for t in range(RADIUS):
        total = total + WEIGHT[t] * (rows(t) + rows(TAPS - 1 - t))
    return total


def kernel(
    ngx, ngy,
    disp, vel, hist, zone, modulus_in, threshold_in, density_in,
    de, v, h, u, tm, rm, out, iy, sx0, pyi,
    z, fys, fx, fy, er, e, yb, xr, ix, ie, pxs, px, pys, py,
    modulus, threshold, density, lsem, ssem, rsem,
):
    gx = lax.axis_index("gx")
    gy = lax.axis_index("gy")
    where_am = {"gx": gx, "gy": gy}
    count = {"gx": ngx, "gy": ngy}

    def reach(axis, step):
        place = where_am[axis] + step
        return (place >= 0) & (place < count[axis])

    local = [
        pltpu.make_async_copy(disp, de.at[:, pl.ds(0, N), pl.ds(0, N), :], lsem.at[0]),
        pltpu.make_async_copy(hist, h, lsem.at[1]),
        pltpu.make_async_copy(zone, z, lsem.at[2]),
        pltpu.make_async_copy(vel, v, lsem.at[3]),
        pltpu.make_async_copy(modulus_in, modulus, lsem.at[4]),
        pltpu.make_async_copy(threshold_in, threshold, lsem.at[5]),
        pltpu.make_async_copy(density_in, density, lsem.at[6]),
    ]
    for copy in local:
        copy.start()

    barrier = pltpu.get_barrier_semaphore()
    partners = jnp.int32(0)
    for axis in ("gx", "gy"):
        for step in (-1, 1):
            ok = reach(axis, step)
            partners = partners + jnp.where(ok, 1, 0)

            @pl.when(ok)
            def _(axis=axis, step=step):
                pl.semaphore_signal(
                    barrier, inc=1, device_id={axis: where_am[axis] + step}, device_id_type=MESH
                )

    made = []

    def remote(src, dst, axis, step):
        k = len(made)
        copy = pltpu.make_async_remote_copy(
            src_ref=src,
            dst_ref=dst,
            send_sem=ssem.at[k],
            recv_sem=rsem.at[k],
            device_id={axis: where_am[axis] + step},
            device_id_type=MESH,
        )
        made.append((copy, axis, step))
        return k

    def start(k):
        copy, axis, step = made[k]
        pl.when(reach(axis, step))(copy.start)

    def far(step):
        return lax.rem(gx, 4) == (3 if step > 0 else 0)

    def start_far(k):
        copy, axis, step = made[k]
        pl.when(reach(axis, step) & far(step))(copy.start)

    def start_near(k):
        copy, axis, step = made[k]
        pl.when(reach(axis, step) & jnp.logical_not(far(step)))(copy.start)

    def arrived(k):
        copy, axis, step = made[k]
        pl.when(reach(axis, -step))(copy.wait_recv)

    def left(k):
        copy, axis, step = made[k]
        pl.when(reach(axis, step))(copy.wait_send)

    def rows(ref, first, number):
        return ref.at[pl.ds(first * N, number * N), :]

    front_x = remote(de.at[:, 0, pl.ds(0, N), :], fx, "gx", -1)
    front_y = remote(fys, fy, "gy", -1)
    part_x = []
    for c in range(3):
        src = e.at[c, pl.ds(25, 23)]
        part_x.append(
            (
                remote(src, e.at[c, pl.ds(1, 23)], "gx", 1),
                remote(src, e.at[c, pl.ds(49, 23)], "gx", -1),
            )
        )
    last_x = (
        remote(e.at[:, 48], e.at[:, 24], "gx", 1),
        remote(e.at[:, 48], e.at[:, 72], "gx", -1),
        remote(e.at[:, 48], e.at[:, 0], "gx", 2),
    )
    part_y = []
    for c in range(3):
        src = rows(yb, 25 + c * CH, CH)
        part_y.append(
            (
                remote(src, rows(yb, 1 + c * CH, CH), "gy", 1),
                remote(src, rows(yb, 49 + c * CH, CH), "gy", -1),
            )
        )
    edge_y = (
        remote(rows(yb, 48, 1), rows(yb, 0, 1), "gy", 2),
        remote(xr.at[pl.ds(N, N), :], xr.at[pl.ds(0, N), :], "gy", 1),
        remote(xr.at[pl.ds(N, N), :], xr.at[pl.ds(2 * N, N), :], "gy", -1),
    )
    face_x = remote(pxs, px, "gx", 1)
    face_y = remote(pys, py, "gy", 1)

    zeros = functools.partial(jnp.zeros, dtype=F32)

    @pl.when(gx == 0)
    def _():
        e[:, 0:25] = zeros((3, 25, CH, DEPTH))
        px[0:3] = zeros((3, N, DEPTH))
        px[3] = zeros((N, DEPTH)) + 1.0

    @pl.when(gx == 1)
    def _():
        e[:, 0] = zeros((3, CH, DEPTH))

    @pl.when(gx == ngx - 1)
    def _():
        e[:, 49:73] = zeros((3, 24, CH, DEPTH))
        fx[...] = zeros((3, N, DEPTH))

    @pl.when(gy == 0)
    def _():
        yb[0 : 25 * N] = zeros((25 * N, DEPTH))
        xr[0:N] = zeros((N, DEPTH))
        py[0:3] = zeros((3, N, DEPTH))
        py[3] = zeros((N, DEPTH)) + 1.0

    @pl.when(gy == 1)
    def _():
        yb[0:N] = zeros((N, DEPTH))

    @pl.when(gy == ngy - 1)
    def _():
        yb[49 * N : 73 * N] = zeros((24 * N, DEPTH))
        xr[2 * N : 3 * N] = zeros((N, DEPTH))
        fy[...] = zeros((3, N, DEPTH))

    left_z = lax.broadcasted_iota(jnp.int32, (DEPTH, DEPTH), 0)
    right_z = lax.broadcasted_iota(jnp.int32, (DEPTH, DEPTH), 1)
    band_z = band(right_z - left_z) / coverage(right_z, DEPTH)
    place = lax.broadcasted_iota(jnp.int32, (25, CH, DEPTH), 0) - 1
    ix[...] = 1.0 / coverage(gx * N + place, ngx * N)
    place = lax.broadcasted_iota(jnp.int32, (N, DEPTH), 0)
    iy[...] = 1.0 / coverage(gy * N + place, ngy * N)
    edge = lax.broadcasted_iota(jnp.int32, (CH, DEPTH), 0) - 1
    ie[...] = 1.0 / coverage(gy * N + edge, ngy * N)

    def along_z(block):
        shape = block.shape
        flat = block.reshape(-1, DEPTH)
        return jnp.dot(flat, band_z, precision=HIGHEST, preferred_element_type=F32).reshape(shape)

    def gradients(i, y0, y1):
        lane = lax.broadcasted_iota(jnp.int32, (y1 - y0, DEPTH), 1)
        centre = [de[j, i, y0:y1, :] for j in range(3)]
        ahead = [
            [de[j, i + 1, y0:y1, :] for j in range(3)],
            [de[j, i, y0 + 1 : y1 + 1, :] for j in range(3)],
            [jnp.where(lane < DEPTH - 1, pltpu.roll(centre[j], DEPTH - 1, 1), 0.0) for j in range(3)],
        ]
        return [[ahead[a][j] - centre[j] for j in range(3)] for a in range(3)]

    def equivalent(i, y0, y1):
        g = gradients(i, y0, y1)
        xy, xz, yz = g[0][1] + g[1][0], g[0][2] + g[2][0], g[1][2] + g[2][1]
        squares = g[0][0] * g[0][0] + g[1][1] * g[1][1] + g[2][2] * g[2][2]
        squares = squares + 0.5 * (xy * xy + xz * xz + yz * yz)
        root = jnp.sqrt(squares)
        for c in range(y0 // CH, y1 // CH):
            er[c, i] = root[c * CH - y0 : (c + 1) * CH - y0]

    local[0].wait()
    for j in range(3):
        fys[j] = de[j, 0:N, 0, :]

    def early(i, carry):
        equivalent(i, 0, 16)
        return carry

    lax.fori_loop(0, N - 1, early, 0, unroll=True)
    e[0:2, 25:48] = along_z(er[0:2, 0:23])

    pl.semaphore_wait(barrier, partners)
    start(front_x)
    start(front_y)
    for c in range(2):
        for k in part_x[c]:
            start_far(k)

    for k in (1, 2, 4, 5, 6):
        local[k].wait()

    def material(i, carry):
        zz = z[i]
        bits = [(zz & 1) != 0, (zz & 2) != 0, (zz & 4) != 0]
        tm[i] = lookup(bits, threshold)
        rm[i] = 0.1 / lookup(bits, density)
        u[5, i] = lookup(bits, modulus)
        return carry

    lax.fori_loop(0, N, material, 0, unroll=4)

    @pl.when(lax.rem(gy, 2) == 0)
    def _():
        for k in part_x[0]:
            start_near(k)

    arrived(front_x)

    @pl.when(lax.rem(gy, 2) == 1)
    def _():
        for k in part_x[0]:
            start_near(k)

    arrived(front_y)
    for j in range(3):
        de[j, N, 0:N, :] = fx[j]
        de[j, 0:N, N, :] = fy[j]

    def late(i, carry):
        equivalent(i, 16, 24)
        return carry

    equivalent(N - 1, 0, N)
    e[:, 48] = along_z(er[:, N - 1])
    for k in last_x:
        start(k)
    lax.fori_loop(0, N - 1, late, 0, unroll=True)
    e[2, 25:48] = along_z(er[2, 0:23])
    for k in part_x[2]:
        start_far(k)
    for k in part_x[1]:
        start_near(k)
    for k in part_x[2]:
        start_near(k)

    def undamaged(i, carry):
        g = gradients(i, 0, N)
        mu = u[5, i]
        trace = mu * (g[0][0] + g[1][1] + g[2][2])
        xy, yy, yz = mu * (g[0][1] + g[1][0]), trace + 2.0 * mu * g[1][1], mu * (g[1][2] + g[2][1])
        u[0, i] = trace + 2.0 * mu * g[0][0]
        u[1, i] = xy
        u[2, i] = mu * (g[0][2] + g[2][0])
        u[3, i] = yy
        u[4, i] = yz
        u[5, i] = trace + 2.0 * mu * g[2][2]
        return carry

    lax.fori_loop(0, N, undamaged, 0, unroll=4)
    limit = tm[N - 1]
    scale = limit * jnp.exp(0.5 * limit)
    for k in range(3):
        pxs[k] = scale * u[k, N - 1]
    pxs[3] = jnp.maximum(h[N - 1], limit)
    limit = tm[0:N, N - 1, :]
    scale = limit * jnp.exp(0.5 * limit)
    for k, source in enumerate((1, 3, 4)):
        pys[k] = scale * u[source, 0:N, N - 1, :]
    pys[3] = jnp.maximum(h[0:N, N - 1, :], limit)

    nothing = zeros((1, CH, DEPTH))

    def middle_rows(c, t):
        if t == 0:
            return jnp.concatenate([nothing, e[c, 1:25]])
        return e[c, t : t + 25]

    for c in range(3):
        for k in part_x[c]:
            arrived(k)
        if c == 0:
            arrived(last_x[0])
            arrived(last_x[1])
        middle = taps(functools.partial(middle_rows, c)) * ix[...]
        xr[N + c * CH : N + (c + 1) * CH, :] = middle[0]
        for i in range(N):
            yb[pl.ds((25 + c * CH) * N + i, CH, stride=N), :] = middle[i + 1]
        for k in part_y[c]:
            start(k)
    start(face_x)
    start(face_y)
    start(edge_y[0])
    arrived(last_x[2])
    for c in range(3):
        xr[N + c * CH : N + (c + 1) * CH, :] += WEIGHT[0] * ix[0] * e[c, 0]
    start(edge_y[1])
    start(edge_y[2])

    def gather(first, number, fresh):
        def group(g, carry):
            off = pl.multiple_of(g * CH, CH)
            source = jnp.stack([yb[pl.ds((first + k) * N + off, CH), :] for k in range(number)])
            if fresh:
                total = jnp.zeros((25, CH, DEPTH), F32)
            else:
                total = jnp.stack([out[pl.ds(m * N + off, CH), :] for m in range(25)])
            for t in range(TAPS):
                lo, hi = max(0, first - t), min(25, first + number - t)
                if lo < hi:
                    part = total[lo:hi] + WEIGHT[t] * source[lo + t - first : hi + t - first]
                    pieces = [total[:lo]] * (lo > 0) + [part] + [total[hi:]] * (hi < 25)
                    total = jnp.concatenate(pieces) if len(pieces) > 1 else part
            for m in range(25):
                out[pl.ds(m * N + off, CH), :] = total[m]
            return carry

        lax.fori_loop(0, N // CH, group, 0)

    gather(25, N, True)
    for c in range(3):
        for k in part_y[c]:
            arrived(k)
        gather(1 + c * CH, CH, False)
        gather(49 + c * CH, CH, False)
    for k in edge_y:
        arrived(k)
    out[0:N] += WEIGHT[0] * yb[0:N]

    arrived(face_x)
    arrived(face_y)

    def intact(least, average):
        bounded = jnp.maximum(least, average)
        return jnp.exp(-0.5 * bounded) / bounded

    row = lax.broadcasted_iota(jnp.int32, (N, 3 * N), 0)
    col = lax.broadcasted_iota(jnp.int32, (N, 3 * N), 1)
    weights = band(col - N - row) / coverage(gy * N + row, ngy * N)
    average_x = jnp.dot(weights, xr[...], precision=HIGHEST, preferred_element_type=F32)
    whole_x = intact(px[3], average_x)
    whole_y = intact(py[3], out[0:N, :] * ie[0:1, :])
    for j in range(3):
        pyi[j] = whole_y * py[j]
        sx0[j] = whole_x * px[j]
    local[3].wait()
    for k in range(len(made)):
        left(k)


PARTS = 4


def finish(de, v, h, u, tm, rm, out, iy, sx0, pyi, nd_out, nv_out, nh_out, nd, nv, nh, sem):
    lane = lax.broadcasted_iota(jnp.int32, (N, DEPTH), 1)
    sub = lax.broadcasted_iota(jnp.int32, (N, DEPTH), 0)

    def row(i, before):
        average = out[pl.ds(N + i, N, stride=N), :] * iy[...]
        top = jnp.maximum(h[i], average)
        nh[i] = top
        limit = tm[i]
        bounded = jnp.maximum(top, limit)
        whole = limit / bounded * jnp.exp(-0.5 * (bounded - limit))
        s = [whole * u[k, i] for k in range(6)]
        sx, sy, sz = (s[0], s[1], s[2]), (s[1], s[3], s[4]), (s[2], s[4], s[5])
        rate = rm[i]
        for j in range(3):
            back_y = jnp.where(sub > 0, pltpu.roll(sy[j], 1, 0), pyi[j, pl.ds(i, 1), :])
            back_z = jnp.where(lane > 0, pltpu.roll(sz[j], 1, 1), 0.0)
            force = sx[j] - before[j] + (sy[j] - back_y) + (sz[j] - back_z)
            speed = v[j, i] + rate * force
            nv[j, i] = speed
            nd[j, i] = de[j, i, 0:N, :] + 0.1 * speed
        return sx

    copies = []
    carry = tuple(sx0[j] for j in range(3))
    size = N // PARTS
    for part in range(PARTS):
        carry = lax.fori_loop(part * size, (part + 1) * size, row, carry, unroll=size)
        span = pl.ds(part * size, size)
        for k, (source, target) in enumerate(
            ((nd.at[:, span], nd_out.at[:, span]), (nv.at[:, span], nv_out.at[:, span]), (nh.at[span], nh_out.at[span]))
        ):
            copies.append(pltpu.make_async_copy(source, target, sem.at[3 * part + k]))
            copies[-1].start()
    for copy in copies:
        copy.wait()


COPIES = 22


def body(ngx, ngy, displacement, velocity, history, zone, zone_modulus, zone_threshold, zone_density):
    block = (N, N, DEPTH)
    plane = (N, DEPTH)
    whole = pl.BlockSpec(memory_space=pltpu.VMEM)
    fixed = pl.BlockSpec(memory_space=pltpu.HBM)
    vmem = lambda *shape: pltpu.VMEM(shape, F32)
    hold = lambda array: pltpu.with_memory_space_constraint(array, pltpu.HBM)
    results = pl.pallas_call(
        functools.partial(kernel, ngx, ngy),
        out_shape=(
            vmem(3, N + 1, 32, DEPTH),
            vmem(3, *block),
            vmem(*block),
            vmem(6, *block),
            vmem(*block),
            vmem(*block),
            vmem(25 * N, DEPTH),
            vmem(*plane),
            vmem(3, *plane),
            vmem(3, *plane),
        ),
        in_specs=[fixed] * 7,
        out_specs=(whole,) * 10,
        scratch_shapes=[
            pltpu.VMEM(block, jnp.int32),
            vmem(3, *plane),
            vmem(3, *plane),
            vmem(3, *plane),
            vmem(3, N, CH, DEPTH),
            vmem(3, 73, CH, DEPTH),
            vmem(73 * N, DEPTH),
            vmem(3 * N, DEPTH),
            vmem(25, CH, DEPTH),
            vmem(CH, DEPTH),
            vmem(4, *plane),
            vmem(4, *plane),
            vmem(4, *plane),
            vmem(4, *plane),
            pltpu.SMEM((8,), F32),
            pltpu.SMEM((8,), F32),
            pltpu.SMEM((8,), F32),
            pltpu.SemaphoreType.DMA((7,)),
            pltpu.SemaphoreType.DMA((COPIES,)),
            pltpu.SemaphoreType.DMA((COPIES,)),
        ],
        compiler_params=pltpu.CompilerParams(
            collective_id=0, has_side_effects=True, vmem_limit_bytes=24 * 1024 * 1024
        ),
    )(*(hold(a) for a in (displacement, velocity, history, zone, zone_modulus, zone_threshold, zone_density)))
    return pl.pallas_call(
        finish,
        out_shape=(
            jax.ShapeDtypeStruct((3, *block), F32),
            jax.ShapeDtypeStruct((3, *block), F32),
            jax.ShapeDtypeStruct(block, F32),
        ),
        in_specs=[whole] * 10,
        out_specs=(fixed,) * 3,
        scratch_shapes=[
            vmem(3, *block),
            vmem(3, *block),
            vmem(*block),
            pltpu.SemaphoreType.DMA((3 * PARTS,)),
        ],
        compiler_params=pltpu.CompilerParams(vmem_limit_bytes=24 * 1024 * 1024),
    )(*(pltpu.with_memory_space_constraint(r, pltpu.VMEM) for r in results))


def solution(mesh):
    return jax.shard_map(
        functools.partial(body, mesh.shape["gx"], mesh.shape["gy"]),
        mesh=mesh,
        in_specs=(
            P(None, "gx", "gy", None),
            P(None, "gx", "gy", None),
            P("gx", "gy", None),
            P("gx", "gy", None),
            P(),
            P(),
            P(),
        ),
        out_specs=(P(None, "gx", "gy", None), P(None, "gx", "gy", None), P("gx", "gy", None)),
        check_vma=False,
    )
```

```python
import functools

import jax
import jax.numpy as jnp
from jax import lax
from jax.experimental import pallas as pl
from jax.experimental.pallas import tpu as pltpu
from jax.sharding import PartitionSpec as P

RADIUS = 24
TAPS = 2 * RADIUS + 1
N = 24
DEPTH = 128
CH = 8
F32 = jnp.float32
MESH = pl.DeviceIdType.MESH
HIGHEST = lax.Precision.HIGHEST

WEIGHT = [1.0 - 0.5 * ((t - RADIUS) / RADIUS) ** 2 for t in range(TAPS)]


def ramp(a):
    return (a * (a + 1) * (2 * a + 1)).astype(F32) * (1.0 / 6.0)


def coverage(place, total):
    low = jnp.minimum(place, RADIUS)
    high = jnp.minimum(total - 1 - place, RADIUS)
    return (low + high + 1).astype(F32) - (ramp(low) + ramp(high)) * (0.5 / RADIUS**2)


def band(offset):
    ratio = offset.astype(F32) * (1.0 / RADIUS)
    return jnp.where(jnp.abs(offset) <= RADIUS, 1.0 - 0.5 * ratio * ratio, 0.0)


def lookup(bits, table):
    level = [table[k] for k in range(8)]
    for bit in bits:
        level = [jnp.where(bit, level[k + 1], level[k]) for k in range(0, len(level), 2)]
    return level[0]


def taps(rows):
    total = rows(RADIUS)
    for t in range(RADIUS):
        total = total + WEIGHT[t] * (rows(t) + rows(TAPS - 1 - t))
    return total


def kernel(
    ngx, ngy,
    disp, vel, hist, zone, modulus_in, threshold_in, density_in,
    de, v, h, u, tm, rm, out, iy, sx0, pyi,
    z, fys, fx, fy, er, e, yb, xr, ix, ie, pxs, px, pys, py,
    modulus, threshold, density, lsem, ssem, rsem,
):
    gx = lax.axis_index("gx")
    gy = lax.axis_index("gy")
    where_am = {"gx": gx, "gy": gy}
    count = {"gx": ngx, "gy": ngy}

    def reach(axis, step):
        place = where_am[axis] + step
        return (place >= 0) & (place < count[axis])

    local = [
        pltpu.make_async_copy(disp, de.at[:, pl.ds(0, N), pl.ds(0, N), :], lsem.at[0]),
        pltpu.make_async_copy(hist, h, lsem.at[1]),
        pltpu.make_async_copy(zone, z, lsem.at[2]),
        pltpu.make_async_copy(vel, v, lsem.at[3]),
        pltpu.make_async_copy(modulus_in, modulus, lsem.at[4]),
        pltpu.make_async_copy(threshold_in, threshold, lsem.at[5]),
        pltpu.make_async_copy(density_in, density, lsem.at[6]),
    ]
    for copy in local:
        copy.start()

    barrier = pltpu.get_barrier_semaphore()
    partners = jnp.int32(0)
    for axis in ("gx", "gy"):
        for step in (-1, 1):
            ok = reach(axis, step)
            partners = partners + jnp.where(ok, 1, 0)

            @pl.when(ok)
            def _(axis=axis, step=step):
                pl.semaphore_signal(
                    barrier, inc=1, device_id={axis: where_am[axis] + step}, device_id_type=MESH
                )

    made = []

    def remote(src, dst, axis, step):
        k = len(made)
        copy = pltpu.make_async_remote_copy(
            src_ref=src,
            dst_ref=dst,
            send_sem=ssem.at[k],
            recv_sem=rsem.at[k],
            device_id={axis: where_am[axis] + step},
            device_id_type=MESH,
        )
        made.append((copy, axis, step))
        return k

    def start(k):
        copy, axis, step = made[k]
        pl.when(reach(axis, step))(copy.start)

    def far(step):
        return lax.rem(gx, 4) == (3 if step > 0 else 0)

    def start_far(k):
        copy, axis, step = made[k]
        pl.when(reach(axis, step) & far(step))(copy.start)

    def start_near(k):
        copy, axis, step = made[k]
        pl.when(reach(axis, step) & jnp.logical_not(far(step)))(copy.start)

    def arrived(k):
        copy, axis, step = made[k]
        pl.when(reach(axis, -step))(copy.wait_recv)

    def left(k):
        copy, axis, step = made[k]
        pl.when(reach(axis, step))(copy.wait_send)

    def rows(ref, first, number):
        return ref.at[pl.ds(first * N, number * N), :]

    front_x = remote(de.at[:, 0, pl.ds(0, N), :], fx, "gx", -1)
    front_y = remote(fys, fy, "gy", -1)
    part_x = []
    for c in range(3):
        src = e.at[c, pl.ds(25, 23)]
        part_x.append(
            (
                remote(src, e.at[c, pl.ds(1, 23)], "gx", 1),
                remote(src, e.at[c, pl.ds(49, 23)], "gx", -1),
            )
        )
    last_x = (
        remote(e.at[:, 48], e.at[:, 24], "gx", 1),
        remote(e.at[:, 48], e.at[:, 72], "gx", -1),
        remote(e.at[:, 48], e.at[:, 0], "gx", 2),
    )
    part_y = []
    for c in range(3):
        src = rows(yb, 25 + c * CH, CH)
        part_y.append(
            (
                remote(src, rows(yb, 1 + c * CH, CH), "gy", 1),
                remote(src, rows(yb, 49 + c * CH, CH), "gy", -1),
            )
        )
    edge_y = (
        remote(rows(yb, 48, 1), rows(yb, 0, 1), "gy", 2),
        remote(xr.at[pl.ds(N, N), :], xr.at[pl.ds(0, N), :], "gy", 1),
        remote(xr.at[pl.ds(N, N), :], xr.at[pl.ds(2 * N, N), :], "gy", -1),
    )
    face_x = remote(pxs, px, "gx", 1)
    face_y = remote(pys, py, "gy", 1)

    zeros = functools.partial(jnp.zeros, dtype=F32)

    @pl.when(gx == 0)
    def _():
        e[:, 0:25] = zeros((3, 25, CH, DEPTH))
        px[0:3] = zeros((3, N, DEPTH))
        px[3] = zeros((N, DEPTH)) + 1.0

    @pl.when(gx == 1)
    def _():
        e[:, 0] = zeros((3, CH, DEPTH))

    @pl.when(gx == ngx - 1)
    def _():
        e[:, 49:73] = zeros((3, 24, CH, DEPTH))
        fx[...] = zeros((3, N, DEPTH))

    @pl.when(gy == 0)
    def _():
        yb[0 : 25 * N] = zeros((25 * N, DEPTH))
        xr[0:N] = zeros((N, DEPTH))
        py[0:3] = zeros((3, N, DEPTH))
        py[3] = zeros((N, DEPTH)) + 1.0

    @pl.when(gy == 1)
    def _():
        yb[0:N] = zeros((N, DEPTH))

    @pl.when(gy == ngy - 1)
    def _():
        yb[49 * N : 73 * N] = zeros((24 * N, DEPTH))
        xr[2 * N : 3 * N] = zeros((N, DEPTH))
        fy[...] = zeros((3, N, DEPTH))

    left_z = lax.broadcasted_iota(jnp.int32, (DEPTH, DEPTH), 0)
    right_z = lax.broadcasted_iota(jnp.int32, (DEPTH, DEPTH), 1)
    band_z = band(right_z - left_z) / coverage(right_z, DEPTH)
    place = lax.broadcasted_iota(jnp.int32, (25, CH, DEPTH), 0) - 1
    ix[...] = 1.0 / coverage(gx * N + place, ngx * N)
    place = lax.broadcasted_iota(jnp.int32, (N, DEPTH), 0)
    iy[...] = 1.0 / coverage(gy * N + place, ngy * N)
    edge = lax.broadcasted_iota(jnp.int32, (CH, DEPTH), 0) - 1
    ie[...] = 1.0 / coverage(gy * N + edge, ngy * N)

    def along_z(block):
        shape = block.shape
        flat = block.reshape(-1, DEPTH)
        return jnp.dot(flat, band_z, precision=HIGHEST, preferred_element_type=F32).reshape(shape)

    def gradients(i, y0, y1):
        lane = lax.broadcasted_iota(jnp.int32, (y1 - y0, DEPTH), 1)
        centre = [de[j, i, y0:y1, :] for j in range(3)]
        ahead = [
            [de[j, i + 1, y0:y1, :] for j in range(3)],
            [de[j, i, y0 + 1 : y1 + 1, :] for j in range(3)],
            [jnp.where(lane < DEPTH - 1, pltpu.roll(centre[j], DEPTH - 1, 1), 0.0) for j in range(3)],
        ]
        return [[ahead[a][j] - centre[j] for j in range(3)] for a in range(3)]

    def equivalent(i, y0, y1):
        g = gradients(i, y0, y1)
        xy, xz, yz = g[0][1] + g[1][0], g[0][2] + g[2][0], g[1][2] + g[2][1]
        squares = g[0][0] * g[0][0] + g[1][1] * g[1][1] + g[2][2] * g[2][2]
        squares = squares + 0.5 * (xy * xy + xz * xz + yz * yz)
        root = jnp.sqrt(squares)
        for c in range(y0 // CH, y1 // CH):
            er[c, i] = root[c * CH - y0 : (c + 1) * CH - y0]

    local[0].wait()
    for j in range(3):
        fys[j] = de[j, 0:N, 0, :]

    def early(i, carry):
        equivalent(i, 0, 16)
        return carry

    lax.fori_loop(0, N - 1, early, 0, unroll=True)
    e[0:2, 25:48] = along_z(er[0:2, 0:23])

    pl.semaphore_wait(barrier, partners)
    start(front_x)
    start(front_y)
    for c in range(2):
        for k in part_x[c]:
            start_far(k)

    for k in (1, 2, 4, 5, 6):
        local[k].wait()

    def material(i, carry):
        zz = z[i]
        bits = [(zz & 1) != 0, (zz & 2) != 0, (zz & 4) != 0]
        tm[i] = lookup(bits, threshold)
        rm[i] = 0.1 / lookup(bits, density)
        u[5, i] = lookup(bits, modulus)
        return carry

    lax.fori_loop(0, N, material, 0, unroll=4)

    @pl.when(lax.rem(gy, 2) == 0)
    def _():
        for k in part_x[0]:
            start_near(k)

    arrived(front_x)

    @pl.when(lax.rem(gy, 2) == 1)
    def _():
        for k in part_x[0]:
            start_near(k)

    arrived(front_y)
    for j in range(3):
        de[j, N, 0:N, :] = fx[j]
        de[j, 0:N, N, :] = fy[j]

    def late(i, carry):
        equivalent(i, 16, 24)
        return carry

    equivalent(N - 1, 0, N)
    e[:, 48] = along_z(er[:, N - 1])
    for k in last_x:
        start(k)
    lax.fori_loop(0, N - 1, late, 0, unroll=True)
    e[2, 25:48] = along_z(er[2, 0:23])
    for k in part_x[2]:
        start_far(k)
    for k in part_x[1]:
        start_near(k)
    for k in part_x[2]:
        start_near(k)

    def undamaged(i, carry):
        g = gradients(i, 0, N)
        mu = u[5, i]
        trace = mu * (g[0][0] + g[1][1] + g[2][2])
        xy, yy, yz = mu * (g[0][1] + g[1][0]), trace + 2.0 * mu * g[1][1], mu * (g[1][2] + g[2][1])
        u[0, i] = trace + 2.0 * mu * g[0][0]
        u[1, i] = xy
        u[2, i] = mu * (g[0][2] + g[2][0])
        u[3, i] = yy
        u[4, i] = yz
        u[5, i] = trace + 2.0 * mu * g[2][2]
        return carry

    lax.fori_loop(0, N, undamaged, 0, unroll=4)
    limit = tm[N - 1]
    scale = limit * jnp.exp(0.5 * limit)
    for k in range(3):
        pxs[k] = scale * u[k, N - 1]
    pxs[3] = jnp.maximum(h[N - 1], limit)
    limit = tm[0:N, N - 1, :]
    scale = limit * jnp.exp(0.5 * limit)
    for k, source in enumerate((1, 3, 4)):
        pys[k] = scale * u[source, 0:N, N - 1, :]
    pys[3] = jnp.maximum(h[0:N, N - 1, :], limit)
    start_near(face_x)

    nothing = zeros((1, CH, DEPTH))

    def middle_rows(c, t):
        if t == 0:
            return jnp.concatenate([nothing, e[c, 1:25]])
        return e[c, t : t + 25]

    for c in range(3):
        for k in part_x[c]:
            arrived(k)
        if c == 0:
            arrived(last_x[0])
            arrived(last_x[1])
        middle = taps(functools.partial(middle_rows, c)) * ix[...]
        xr[N + c * CH : N + (c + 1) * CH, :] = middle[0]
        for i in range(N):
            yb[pl.ds((25 + c * CH) * N + i, CH, stride=N), :] = middle[i + 1]
        for k in part_y[c]:
            start(k)
    start(face_y)
    start_far(face_x)
    start(edge_y[0])
    arrived(last_x[2])
    for c in range(3):
        xr[N + c * CH : N + (c + 1) * CH, :] += WEIGHT[0] * ix[0] * e[c, 0]
    start(edge_y[1])
    start(edge_y[2])

    def gather(blocks, fresh):
        def group(g, carry):
            off = pl.multiple_of(g * CH, CH)
            if fresh:
                total = jnp.zeros((25, CH, DEPTH), F32)
            else:
                total = jnp.stack([out[pl.ds(m * N + off, CH), :] for m in range(25)])
            for first, number in blocks:
                source = jnp.stack([yb[pl.ds((first + k) * N + off, CH), :] for k in range(number)])
                for t in range(TAPS):
                    lo, hi = max(0, first - t), min(25, first + number - t)
                    if lo < hi:
                        part = total[lo:hi] + WEIGHT[t] * source[lo + t - first : hi + t - first]
                        pieces = [total[:lo]] * (lo > 0) + [part] + [total[hi:]] * (hi < 25)
                        total = jnp.concatenate(pieces) if len(pieces) > 1 else part
            for m in range(25):
                out[pl.ds(m * N + off, CH), :] = total[m]
            return carry

        lax.fori_loop(0, N // CH, group, 0, unroll=not fresh)

    gather([(25, N)], True)
    for c in range(3):
        for k in part_y[c]:
            arrived(k)
        gather([(1 + c * CH, CH), (49 + c * CH, CH)], False)
    for k in edge_y:
        arrived(k)
    out[0:N] += WEIGHT[0] * yb[0:N]

    arrived(face_x)
    arrived(face_y)

    def intact(least, average):
        bounded = jnp.maximum(least, average)
        return jnp.exp(-0.5 * bounded) / bounded

    row = lax.broadcasted_iota(jnp.int32, (N, 3 * N), 0)
    col = lax.broadcasted_iota(jnp.int32, (N, 3 * N), 1)
    weights = band(col - N - row) / coverage(gy * N + row, ngy * N)
    average_x = jnp.dot(weights, xr[...], precision=HIGHEST, preferred_element_type=F32)
    whole_x = intact(px[3], average_x)
    whole_y = intact(py[3], out[0:N, :] * ie[0:1, :])
    for j in range(3):
        pyi[j] = whole_y * py[j]
        sx0[j] = whole_x * px[j]
    local[3].wait()
    for k in range(len(made)):
        left(k)


PARTS = 6


def finish(de, v, h, u, tm, rm, out, iy, sx0, pyi, nd_out, nv_out, nh_out, nd, nv, nh, sem):
    lane = lax.broadcasted_iota(jnp.int32, (N, DEPTH), 1)
    sub = lax.broadcasted_iota(jnp.int32, (N, DEPTH), 0)

    def row(i, before):
        average = out[pl.ds(N + i, N, stride=N), :] * iy[...]
        top = jnp.maximum(h[i], average)
        nh[i] = top
        limit = tm[i]
        bounded = jnp.maximum(top, limit)
        whole = limit / bounded * jnp.exp(-0.5 * (bounded - limit))
        s = [whole * u[k, i] for k in range(6)]
        sx, sy, sz = (s[0], s[1], s[2]), (s[1], s[3], s[4]), (s[2], s[4], s[5])
        rate = rm[i]
        for j in range(3):
            back_y = jnp.where(sub > 0, pltpu.roll(sy[j], 1, 0), pyi[j, pl.ds(i, 1), :])
            back_z = jnp.where(lane > 0, pltpu.roll(sz[j], 1, 1), 0.0)
            force = sx[j] - before[j] + (sy[j] - back_y) + (sz[j] - back_z)
            speed = v[j, i] + rate * force
            nv[j, i] = speed
            nd[j, i] = de[j, i, 0:N, :] + 0.1 * speed
        return sx

    copies = []
    carry = tuple(sx0[j] for j in range(3))
    size = N // PARTS
    for part in range(PARTS):
        carry = lax.fori_loop(part * size, (part + 1) * size, row, carry, unroll=size)
        span = pl.ds(part * size, size)
        for k, (source, target) in enumerate(
            ((nd.at[:, span], nd_out.at[:, span]), (nv.at[:, span], nv_out.at[:, span]), (nh.at[span], nh_out.at[span]))
        ):
            copies.append(pltpu.make_async_copy(source, target, sem.at[3 * part + k]))
            copies[-1].start()
    for copy in copies:
        copy.wait()


COPIES = 22


def body(ngx, ngy, displacement, velocity, history, zone, zone_modulus, zone_threshold, zone_density):
    block = (N, N, DEPTH)
    plane = (N, DEPTH)
    whole = pl.BlockSpec(memory_space=pltpu.VMEM)
    fixed = pl.BlockSpec(memory_space=pltpu.HBM)
    vmem = lambda *shape: pltpu.VMEM(shape, F32)
    hold = lambda array: pltpu.with_memory_space_constraint(array, pltpu.HBM)
    results = pl.pallas_call(
        functools.partial(kernel, ngx, ngy),
        out_shape=(
            vmem(3, N + 1, 32, DEPTH),
            vmem(3, *block),
            vmem(*block),
            vmem(6, *block),
            vmem(*block),
            vmem(*block),
            vmem(26 * N, DEPTH),
            vmem(*plane),
            vmem(3, *plane),
            vmem(3, *plane),
        ),
        in_specs=[fixed] * 7,
        out_specs=(whole,) * 10,
        scratch_shapes=[
            pltpu.VMEM(block, jnp.int32),
            vmem(3, *plane),
            vmem(3, *plane),
            vmem(3, *plane),
            vmem(3, N, CH, DEPTH),
            vmem(3, 73, CH, DEPTH),
            vmem(73 * N, DEPTH),
            vmem(3 * N, DEPTH),
            vmem(25, CH, DEPTH),
            vmem(CH, DEPTH),
            vmem(4, *plane),
            vmem(4, *plane),
            vmem(4, *plane),
            vmem(4, *plane),
            pltpu.SMEM((8,), F32),
            pltpu.SMEM((8,), F32),
            pltpu.SMEM((8,), F32),
            pltpu.SemaphoreType.DMA((7,)),
            pltpu.SemaphoreType.DMA((COPIES,)),
            pltpu.SemaphoreType.DMA((COPIES,)),
        ],
        compiler_params=pltpu.CompilerParams(
            collective_id=0, has_side_effects=True, vmem_limit_bytes=24 * 1024 * 1024
        ),
    )(*(hold(a) for a in (displacement, velocity, history, zone, zone_modulus, zone_threshold, zone_density)))
    return pl.pallas_call(
        finish,
        out_shape=(
            jax.ShapeDtypeStruct((3, *block), F32),
            jax.ShapeDtypeStruct((3, *block), F32),
            jax.ShapeDtypeStruct(block, F32),
        ),
        in_specs=[whole] * 10,
        out_specs=(fixed,) * 3,
        scratch_shapes=[
            vmem(3, *block),
            vmem(3, *block),
            vmem(*block),
            pltpu.SemaphoreType.DMA((3 * PARTS,)),
        ],
        compiler_params=pltpu.CompilerParams(vmem_limit_bytes=24 * 1024 * 1024),
    )(*(pltpu.with_memory_space_constraint(r, pltpu.VMEM) for r in results))


def solution(mesh):
    return jax.shard_map(
        functools.partial(body, mesh.shape["gx"], mesh.shape["gy"]),
        mesh=mesh,
        in_specs=(
            P(None, "gx", "gy", None),
            P(None, "gx", "gy", None),
            P("gx", "gy", None),
            P("gx", "gy", None),
            P(),
            P(),
            P(),
        ),
        out_specs=(P(None, "gx", "gy", None), P(None, "gx", "gy", None), P("gx", "gy", None)),
        check_vma=False,
    )
```
